32 devices in a mesh: sec: 16 (over z, y, x), band: 2 (over core).
Axes of the slice: x: 2, y: 2, z: 4, core: 2. Of those that a mesh axis runs over, the one named last changes fastest.
Arguments:
- velocity: float32 [3, 32, 256, 512], P(None, 'band', 'sec'), may hold values from -6 to 6
- crop_level: int32 [16, 2, 16], P('sec', 'band'), may hold values from 0 to 12
- crop_x: int32 [16, 2, 16], P('sec', 'band'), may hold values from 0 to 4
- crop_y: int32 [16, 2, 16], P('sec', 'band'), may hold values from 0 to 248
- live_count: int32 [32], P(('sec', 'band')), may hold values from 1 to 16, 320 in all
- w_first: float32 [27, 64, 3], replicated, may hold values from -0.625 to 0.625
- norm_gain: float32 [64], replicated, may hold values from 0.25 to 1.75
- norm_shift: float32 [64], replicated, may hold values from -3 to 3
- w_middle: float32 [27, 64, 64], replicated, may hold values from -0.15625 to 0.15625
- w_last: float32 [27, 6, 64], replicated, may hold values from -0.15625 to 0.15625
Outputs:
- velocity_next: float32 [3, 32, 256, 512], P(None, 'band', 'sec')
- new_first: float32 [27, 64, 3], replicated
- new_gain: float32 [64], replicated
- new_shift: float32 [64], replicated
- new_middle: float32 [27, 64, 64], replicated
- new_last: float32 [27, 6, 64], replicated
- loss: float32 [], replicated
The draws below stay inside these ranges and needn't reach their ends.
Inputs may be any that keep to these rules, and one draw needn't show every extreme that they name: `live_count`: the counts sum to 320.
All inputs are finite; a program needn't handle non-finite values. No bound on the sum of `live_count` on one device may be relied on, other than what follows from the above.
Results may differ from the reference program's by a relative error of at most 0.00043.
Values may be sent and summed in bfloat16 or wider, within the bound.
No kernel may reach another device: no remote copies, remote signals or barrier semaphores. Data moves between devices by JAX's collectives and lax.ppermute only.
A program may use at most 320 MiB of HBM per device.

```python
import math
import jax
import jax.numpy as jnp
import numpy as np
from jax import lax

CX = 16
CY = 512
LZ = 16
PZ = 4
PX = 4
PY = 8
CH = 64
TAPS = 27
SECS = 16
BANDS = 2
SAMPLES_DEV = 16
TRAINERS = 32
LIVE = 320
NX = 256
LEV = 32


def place_ends(array, rng, low, top_value):
    place = [jax.random.randint(jax.random.fold_in(rng, axis), (), 0, length) for axis, length in enumerate(array.shape)]
    main_axis = array.shape.index(max(array.shape))
    beside = place[:main_axis] + [(place[main_axis] + 1) % array.shape[main_axis]] + place[main_axis + 1:]
    return array.at[tuple(place)].set(low).at[tuple(beside)].set(top_value)


def block_levels(stream_key, shape, cuts, least, high):
    loudness = 1.0
    for dim, shards_of in cuts:
        steps = jax.random.uniform(jax.random.fold_in(jax.random.fold_in(stream_key, 6), dim), (shards_of,), jnp.float32, least / len(cuts), high / len(cuts))
        loudness = loudness * jnp.repeat(jnp.exp(steps), shape[dim] // shards_of).reshape((-1,) + (1,) * (len(shape) - 1 - dim))
    return loudness


def profile(amount, total, limit, skew):
    weights = [(1 << 20) // math.isqrt(grade ** skew) + 1 for grade in range(2, amount + 1)]
    spare, holding = total - limit - (amount - 1), [1] * (amount - 1)
    while spare > 0:
        candidates = [i for i in range(amount - 1) if holding[i] < limit]
        whole, budget = sum([weights[i] for i in candidates]), spare
        for i in candidates:
            extra = min(limit - holding[i], max(1, budget * weights[i] // whole), spare)
            holding[i] = holding[i] + extra
            spare = spare - extra
    return np.array([limit] + holding)


def ragged_sizes(rng, number_of, total, bound, lean):
    if number_of == 2:
        one = jax.random.randint(rng, (), max(1, total - bound), min(bound, total - 1) + 1)
        return jnp.stack([one, total - one])
    lengths = jnp.asarray(profile(number_of, total, bound, lean), jnp.int32)
    couples = (number_of - 1) // 2
    donor, receiver = lengths[1:1 + 2 * couples:2], lengths[2:2 + 2 * couples:2]
    room = jnp.minimum(donor - 1, bound - receiver)
    moved = jax.random.randint(jax.random.fold_in(rng, 1), (couples,), 0, 1 << 20) % (room + 1)
    lengths = lengths.at[1:1 + 2 * couples:2].set(donor - moved).at[2:2 + 2 * couples:2].set(receiver + moved)
    return lengths[jax.random.permutation(jax.random.fold_in(rng, 2), number_of)]


def scatter_about(stream_key, shape, scale, limit, shards=(), kind=jnp.bfloat16):
    loudness = block_levels(stream_key, shape, shards, -0.22, 0.18) if shards else 1.0
    array = jax.random.normal(stream_key, shape, jnp.float32) * scale * loudness
    return jnp.minimum(jnp.maximum(array, -limit), limit).astype(kind)


def setup_inputs(seed: int = 0) -> dict:
    arg_keys = jax.random.split(jax.random.key(seed), 11)
    return {
        "velocity": scatter_about(arg_keys[0], (3, LEV, NX, CY), 1.0, 6.0, ((1, 2), (2, 16)), jnp.float32),
        "crop_level": place_ends(jax.random.randint(arg_keys[1], (SECS, BANDS, SAMPLES_DEV), 0, LZ - PZ + 1), jax.random.fold_in(arg_keys[1], 1), 0, LZ - PZ).astype(jnp.int32),
        "crop_x": place_ends(jax.random.randint(arg_keys[2], (SECS, BANDS, SAMPLES_DEV), 0, CX // 2 - PX + 1), jax.random.fold_in(arg_keys[2], 1), 0, (CX // 2 - PX + 1) - 1).astype(jnp.int32),
        "crop_y": place_ends(jax.random.randint(arg_keys[3], (SECS, BANDS, SAMPLES_DEV), 0, CY // 2 - PY + 1), jax.random.fold_in(arg_keys[3], 1), 0, (CY // 2 - PY + 1) - 1).astype(jnp.int32),
        "live_count": ragged_sizes(arg_keys[4], TRAINERS, LIVE, SAMPLES_DEV, 2).astype(jnp.int32),
        "w_first": scatter_about(arg_keys[5], (TAPS, CH, 3), (3 * TAPS) ** -0.5, 0.625, (), jnp.float32),
        "norm_gain": jnp.clip(1.0 + 0.15 * jax.random.normal(arg_keys[6], (CH,), jnp.float32), 0.25, 1.75),
        "norm_shift": scatter_about(arg_keys[7], (CH,), 0.5, 3.0, (), jnp.float32),
        "w_middle": scatter_about(arg_keys[8], (TAPS, CH, CH), (CH * TAPS) ** -0.5, 0.15625, (), jnp.float32),
        "w_last": scatter_about(arg_keys[9], (TAPS, 6, CH), (CH * TAPS) ** -0.5, 0.15625, (), jnp.float32),
    }


TIME_STEP = 0.2
VISCOSITY = 0.5
LEARNING = 1.0
EPSILON = 1e-05
PAIRS = ((0, 0), (1, 1), (2, 2), (0, 1), (0, 2), (1, 2))

def advance(padded):
    centre = padded[:, 1:-1, 1:-1, :]
    upper = padded[:, 2:, 1:-1, :]
    lower = padded[:, :-2, 1:-1, :]
    eastern = padded[:, 1:-1, 2:, :]
    western = padded[:, 1:-1, :-2, :]
    northern = jnp.roll(centre, -1, axis=3)
    southern = jnp.roll(centre, 1, axis=3)
    laplace = upper + lower + eastern + western + northern + southern - 6.0 * centre
    advect = centre[0:1] * (eastern - western) * 0.5 + centre[1:2] * (northern - southern) * 0.5 + centre[2:3] * (upper - lower) * 0.5
    return centre + TIME_STEP * (VISCOSITY * laplace - advect)

def coarsen(field):
    extent = field.shape
    blocked = field.reshape(extent[:-2] + (extent[-2] // 2, 2, extent[-1] // 2, 2))
    return lax.optimization_barrier(jnp.mean(blocked, axis=(-3, -1)))

def features(velocity):
    averages = coarsen(velocity)
    stresses = [coarsen(velocity[first] * velocity[second]) - averages[first] * averages[second] for first, second in PAIRS]
    return jnp.concatenate([averages, jnp.stack(stresses)], axis=0).astype(jnp.bfloat16)

def convolve(weight, inputs):
    extent = inputs.shape[2]
    margin = PX * PY + PY + 1
    where = jnp.arange(extent, dtype=jnp.int32)
    level_index = where // (PX * PY)
    column = where // PY % PX
    spanwise = where % PY
    padded = jnp.pad(inputs, ((0, 0), (0, 0), (margin, margin)))
    total = jnp.zeros((inputs.shape[0], weight.shape[1], extent), jnp.float32)
    tap_index = 0
    for shift_z in (-1, 0, 1):
        for shift_x in (-1, 0, 1):
            for shift_y in (-1, 0, 1):
                offset = shift_z * PX * PY + shift_x * PY + shift_y
                inside = (level_index + shift_z >= 0) & (level_index + shift_z < PZ) & (column + shift_x >= 0) & (column + shift_x < PX) & (spanwise + shift_y >= 0) & (spanwise + shift_y < PY)
                moved = lax.slice_in_dim(padded, margin + offset, margin + offset + extent, axis=2)
                moved = moved * inside.astype(inputs.dtype)
                total = total + jnp.einsum('oc,scp->sop', weight[tap_index].astype(jnp.float32), moved.astype(jnp.float32))
                tap_index += 1
    return total

def layer_first(weight, scales, shifts, inputs, live_mask, live_points):
    hidden = convolve(weight.astype(jnp.bfloat16), inputs)
    masking = live_mask[:, None, None]
    average = lax.optimization_barrier(jnp.sum(hidden * masking, axis=(0, 2))) / live_points
    centred = hidden - average[None, :, None]
    variance = lax.optimization_barrier(jnp.sum(centred * centred * masking, axis=(0, 2))) / live_points
    normed = centred * lax.rsqrt(variance + EPSILON)[None, :, None] * scales[None, :, None] + shifts[None, :, None]
    return jax.nn.silu(normed).astype(jnp.bfloat16)

def layer_middle(weight, inputs):
    return jax.nn.silu(convolve(weight.astype(jnp.bfloat16), inputs)).astype(jnp.bfloat16)

def layer_last(weight, inputs, target, live_mask, factor):
    output = convolve(weight.astype(jnp.bfloat16), inputs)
    error = (output - target.astype(jnp.float32)) * live_mask[:, None, None]
    return jnp.sum(error * error) * factor

def train_terms(batch, count, w_first, norm_gain, norm_shift, w_middle, w_last, factor):
    inputs = batch[:, :3]
    target = batch[:, 3:]
    live_mask = (jnp.arange(batch.shape[0], dtype=jnp.int32) < count).astype(jnp.float32)
    live_points = count.astype(jnp.float32) * batch.shape[2]
    act_first, back_first = jax.vjp(lambda weight, scales, shifts: layer_first(weight, scales, shifts, inputs, live_mask, live_points), w_first, norm_gain, norm_shift)
    act_middle, back_middle = jax.vjp(layer_middle, w_middle, act_first)
    group_loss, back_last = jax.vjp(lambda weight, hidden: layer_last(weight, hidden, target, live_mask, factor), w_last, act_middle)
    grad_last, cot_middle = back_last(jnp.ones_like(group_loss))
    grad_middle, cot_first = back_middle(cot_middle)
    grad_first, grad_gain, grad_shift = back_first(cot_first)
    return (group_loss, grad_first, grad_gain, grad_shift, grad_middle, grad_last)

def reference(velocity, crop_level, crop_x, crop_y, live_count, w_first, norm_gain, norm_shift, w_middle, w_last):
    padded = jnp.pad(velocity, ((0, 0), (1, 1), (1, 1), (0, 0)))
    velocity_next = advance(padded)
    fields = features(velocity_next)
    sec_index = jnp.arange(SECS, dtype=jnp.int32)[:, None, None]
    band_index = jnp.arange(BANDS, dtype=jnp.int32)[None, :, None]
    start_level = (band_index * LZ + crop_level).reshape(-1).astype(jnp.int32)
    start_column = (sec_index * (CX // 2) + crop_x).reshape(-1).astype(jnp.int32)
    start_row = jnp.broadcast_to(crop_y, (SECS, BANDS, SAMPLES_DEV)).reshape(-1).astype(jnp.int32)

    def cutting(level_at, column_at, row_at):
        return lax.dynamic_slice(fields, (jnp.int32(0), level_at, column_at, row_at), (9, PZ, PX, PY))
    crops = jax.vmap(cutting)(start_level, start_column, start_row)
    crops = crops.reshape(SECS, BANDS, SAMPLES_DEV, 9, PZ * PX * PY)
    batches = jnp.transpose(crops, (2, 1, 0, 3, 4)).reshape(TRAINERS, SECS, 9, PZ * PX * PY)
    factor = jnp.float32(1.0 / (6.0 * PZ * PX * PY * LIVE))
    terms = lax.map(lambda pair: train_terms(pair[0], pair[1], w_first, norm_gain, norm_shift, w_middle, w_last, factor), (batches, live_count))
    loss, grad_first, grad_gain, grad_shift, grad_middle, grad_last = tuple((lax.optimization_barrier(jnp.sum(term, axis=0)) for term in terms))
    return (velocity_next, w_first - LEARNING * grad_first, norm_gain - LEARNING * grad_gain, norm_shift - LEARNING * grad_shift, w_middle - LEARNING * grad_middle, w_last - LEARNING * grad_last, loss)
```

```python
import functools

import jax
import jax.numpy as jnp
from jax import lax
from jax.experimental import pallas as pl
from jax.experimental.pallas import tpu as pltpu
from jax.sharding import PartitionSpec as P

PZ = 4
PX = 4
PY = 8
CH = 64
LANES = 128
KIN = PZ * PX
CHUNK = LANES // PY
FIELD_ROWS = 16
TAP_ROWS = 27 * 8

TIME_STEP = 0.2
VISCOSITY = 0.5
LEARNING = 1.0
EPSILON = 1e-05
PAIRS = ((0, 0), (1, 1), (2, 2), (0, 1), (0, 2), (1, 2))
OFFSETS = (-1, 0, 1)
TAPS = [(dz, dx, dy) for dz in OFFSETS for dx in OFFSETS for dy in OFFSETS]

F32 = jnp.float32
BF16 = jnp.bfloat16
VMEM = pl.BlockSpec(memory_space=pltpu.VMEM)
SMEM = pl.BlockSpec(memory_space=pltpu.SMEM)
ANY = pl.BlockSpec(memory_space=pl.ANY)
PARAMS = pltpu.CompilerParams(vmem_limit_bytes=60 * 1024 * 1024)

MID_TILES = 4
MID_ROWS = 3 * CH
HALF_BASE = MID_TILES * MID_ROWS
PLANE_BASE = HALF_BASE + MID_ROWS // 2
PLANE_STEP = 32
MISC_BASE = PLANE_BASE + 4 * PLANE_STEP + 27
EXCHANGE_ROWS = 1024


def nt(left, right):
    return lax.dot_general(left, right, (((1,), (1,)), ((), ())), preferred_element_type=F32)


def mm(left, right):
    return lax.dot_general(left, right, (((1,), (0,)), ((), ())), preferred_element_type=F32)


def tn(left, right):
    return lax.dot_general(left, right, (((0,), (0,)), ((), ())), preferred_element_type=F32)


def each(number, body):
    if number == 1:
        body(0)
    else:
        lax.fori_loop(0, number, lambda i, c: (body(i), c)[1], 0)


def weights_kernel(wf_ref, wm_ref, wl_ref, w1_ref, w2f_ref, w2b_ref, w3f_ref, w3b_ref, rows):
    rows[...] = jnp.zeros_like(rows)
    for c in range(3):
        rows[pl.ds(c, 27, stride=8), :] = wf_ref[c]
    w1_ref[...] = jnp.transpose(rows[...]).astype(BF16)
    rows[...] = jnp.zeros_like(rows)
    for o in range(6):
        rows[pl.ds(o, 27, stride=8), :] = wl_ref[o]
    w3f_ref[...] = rows[...].astype(BF16)
    w3b_ref[...] = jnp.transpose(rows[...]).astype(BF16)
    for z in range(3):
        taps = [wm_ref[z * 9 + j] for j in range(9)]
        w2f_ref[z * CH : (z + 1) * CH, :] = jnp.concatenate(taps, axis=1).astype(BF16)
        turned = jnp.transpose(jnp.concatenate(taps, axis=0))
        w2b_ref[z * CH : (z + 1) * CH, :] = turned.astype(BF16)


def arrange_weights(wf, wm, wl):
    return pl.pallas_call(
        weights_kernel,
        out_shape=(
            jax.ShapeDtypeStruct((CH, TAP_ROWS), BF16),
            jax.ShapeDtypeStruct((3 * CH, 9 * CH), BF16),
            jax.ShapeDtypeStruct((3 * CH, 9 * CH), BF16),
            jax.ShapeDtypeStruct((TAP_ROWS, CH), BF16),
            jax.ShapeDtypeStruct((CH, TAP_ROWS), BF16),
        ),
        in_specs=[VMEM] * 3,
        out_specs=(VMEM,) * 5,
        scratch_shapes=[pltpu.VMEM((TAP_ROWS, CH), F32)],
        name="arrange_weights",
    )(wf, wm, wl)


def lane_values(values_ref, base, lanes):
    which = (lanes % LANES) // PY
    out = jnp.zeros(lanes.shape, jnp.int32)
    for k in range(CHUNK):
        out = jnp.where(which == k, values_ref[base + k], out)
    return out


def flow_kernel(place_ref, level_ref, cx_ref, cy_ref, v_ref, a_ref, b_ref, c_ref, out_ref, crop_ref, vn, parts, chosen, sems):
    odd = place_ref[0] == 1
    upper_band = place_ref[1] == 1
    _, levels, nx, ny = v_ref.shape
    row = lax.broadcasted_iota(jnp.int32, (nx, ny), 0)
    copies = []
    for l in range(levels):
        centre = [v_ref[c, l] for c in range(3)]
        nxt = []
        for c in range(3):
            first = a_ref[c, l : l + 1, :]
            second = b_ref[c, l : l + 1, :]
            west = jnp.where(odd, first, second)
            east = jnp.where(odd, second, first)
            beyond = c_ref[c]
            if l + 1 < levels:
                upper = v_ref[c, l + 1]
            else:
                upper = jnp.where(upper_band, 0.0, beyond)
            if l > 0:
                lower = v_ref[c, l - 1]
            else:
                lower = jnp.where(upper_band, beyond, 0.0)
            mid = centre[c]
            eastern = jnp.where(row == nx - 1, east, pltpu.roll(mid, nx - 1, 0))
            western = jnp.where(row == 0, west, pltpu.roll(mid, 1, 0))
            northern = pltpu.roll(mid, ny - 1, 1)
            southern = pltpu.roll(mid, 1, 1)
            laplace = upper + lower + eastern + western + northern + southern - 6.0 * mid
            advect = (
                centre[0] * (eastern - western) * 0.5
                + centre[1] * (northern - southern) * 0.5
                + centre[2] * (upper - lower) * 0.5
            )
            new = mid + TIME_STEP * (VISCOSITY * laplace - advect)
            vn[c, l] = new
            nxt.append(new)
        copy = pltpu.make_async_copy(vn.at[:, l], out_ref.at[:, l], sems.at[l])
        copy.start()
        copies.append(copy)
        new = jnp.concatenate(nxt, axis=0)
        high = new.astype(BF16)
        rest = new - high.astype(F32)
        middle = rest.astype(BF16)
        low = (rest - middle.astype(F32)).astype(BF16)
        parts[l * 9 * nx : (l + 1) * 9 * nx, :] = jnp.concatenate([high, middle, low], axis=0)

    lanes = lax.broadcasted_iota(jnp.int32, (1, 2 * LANES), 1)
    position = lax.broadcasted_iota(jnp.int32, (ny, 2 * LANES), 0)
    ch_rows = 9 * PZ * 8
    r = lax.broadcasted_iota(jnp.int32, (ch_rows, KIN * FIELD_ROWS), 0)
    col = lax.broadcasted_iota(jnp.int32, (ch_rows, KIN * FIELD_ROWS), 1)
    channel = r >> 5
    slot = jnp.where(channel < 3, channel, channel + 5)
    goal = ((((r >> 3) & 3) * PX + ((r & 7) >> 1)) * FIELD_ROWS) + slot
    place = jnp.where((col == goal) & ((r & 1) == 0), 1.0, 0.0).astype(BF16)

    def chunk(k):
        base = k * CHUNK
        level_of = lane_values(level_ref, base, lanes)
        x_of = lane_values(cx_ref, base, lanes)
        y_of = lane_values(cy_ref, base, lanes)
        source = 2 * (y_of + lanes % PY) + lanes // LANES
        picks = jnp.where(position == source, 1.0, 0.0).astype(BF16)
        half = levels // 2
        for part in range(2):
            span = half * 9 * nx
            got = mm(parts[part * span : (part + 1) * span, :], picks)
            for i in range(half):
                at = i * 9 * nx
                w = 3 * nx
                chosen[part * half + i] = (got[at : at + w] + got[at + w : at + 2 * w]) + got[at + 2 * w : at + 3 * w]
        rows = [None] * (9 * PZ)
        for l in range(PZ):
            window = []
            for c in range(3):
                take = slice(c * nx, (c + 1) * nx)
                kept = chosen[l, take, :]
                for o in range(1, levels - PZ + 1):
                    kept = jnp.where(level_of == o, chosen[o + l, take, :], kept)
                cells = kept[0 : 2 * PX]
                for o in range(1, nx // 2 - PX + 1):
                    cells = jnp.where(x_of == o, kept[2 * o : 2 * o + 2 * PX], cells)
                window.append(cells)

            def box(cells):
                pair = cells[:, :LANES] + cells[:, LANES:]
                return (pair + pltpu.roll(pair, 2 * PX - 1, 0)) * 0.25

            means = [box(cells) for cells in window]
            for c in range(3):
                rows[c * PZ + l] = means[c]
            for n, (i, j) in enumerate(PAIRS):
                rows[(3 + n) * PZ + l] = box(window[i] * window[j]) - means[i] * means[j]
        fields = jnp.concatenate(rows, axis=0).astype(BF16)
        crop_ref[k] = tn(fields, place).astype(BF16)

    each(crop_ref.shape[0], chunk)
    for copy in copies:
        copy.wait()


def flow_step(place, level, cx, cy, velocity, first, second, beyond):
    chunks = level.shape[0] // CHUNK
    _, levels, nx, ny = velocity.shape
    return pl.pallas_call(
        flow_kernel,
        out_shape=(
            jax.ShapeDtypeStruct(velocity.shape, F32),
            jax.ShapeDtypeStruct((chunks, LANES, KIN * FIELD_ROWS), BF16),
        ),
        in_specs=[SMEM] * 4 + [VMEM] * 4,
        out_specs=(ANY, VMEM),
        scratch_shapes=[
            pltpu.VMEM(velocity.shape, F32),
            pltpu.VMEM((levels * 9 * nx, ny), BF16),
            pltpu.VMEM((levels, 3 * nx, 2 * LANES), F32),
            pltpu.SemaphoreType.DMA((levels,)),
        ],
        compiler_params=PARAMS,
        name="flow_step",
    )(place, level, cx, cy, velocity, first, second, beyond)


def train_kernel(
    factor, count_ref, batch_ref, gain_ref, shift_ref, w1_ref, w2f_ref, w2b_ref, w3f_ref, w3b_ref,
    out_ref, sx, hidden, s2, h2, act2, tap_out, des, dys, dn, flat, g2, small,
):
    chunks = batch_ref.shape[0]
    width = KIN * LANES
    band = PX * LANES
    count = count_ref[0]
    points = count.astype(F32) * (KIN * PY)
    lane = lax.broadcasted_iota(jnp.int32, (1, LANES), 1)
    y = lane % PY
    inside = {-1: y > 0, 1: y < PY - 1}

    def live(k):
        return jnp.where(k * CHUNK + lane // PY < count, 1.0, 0.0)

    def shifted(block, dy):
        if dy == 0:
            return block
        return jnp.where(inside[dy], pltpu.roll(block, (-dy) % LANES, 1), 0.0)

    def at(l, x):
        return slice((l * PX + x) * LANES, (l * PX + x + 1) * LANES)

    def stack_taps(blocks, sign, store):
        moved = {dy: [shifted(block, dy) for block in blocks] for dy in OFFSETS}
        zero = jnp.zeros((8, LANES), F32)
        for l in range(PZ):
            for x in range(PX):
                column = []
                for dz, dx, dy in TAPS:
                    lz, xx = l + sign * dz, x + sign * dx
                    ok = 0 <= lz < PZ and 0 <= xx < PX
                    column.append(moved[sign * dy][lz * PX + xx] if ok else zero)
                store(at(l, x), jnp.concatenate(column, axis=0).astype(BF16))

    def stack_planes(block_of, sign):
        zero = jnp.zeros((CH, LANES), BF16)
        for l in range(PZ):
            for x in range(PX):
                block = block_of(l, x)
                for i, dy in enumerate(OFFSETS):
                    piece = shifted(block, sign * dy).astype(BF16)
                    for j, dx in enumerate(OFFSETS):
                        goal = x - sign * dx
                        if 0 <= goal < PX:
                            s2[(j * 3 + i) * CH : (j * 3 + i + 1) * CH, at(l, goal)] = piece
            for i in range(3):
                for j, dx in enumerate(OFFSETS):
                    edge = {-1: 0, 1: PX - 1}.get(sign * dx)
                    if edge is not None:
                        s2[(j * 3 + i) * CH : (j * 3 + i + 1) * CH, at(l, edge)] = zero

    def plane_products(weights, sign, target):
        for l in range(PZ):
            got = mm(weights[...], s2[:, l * band : (l + 1) * band])
            for i, dz in enumerate(OFFSETS):
                goal = l - sign * dz
                if 0 <= goal < PZ:
                    piece = got[i * CH : (i + 1) * CH]
                    where = slice(goal * band, (goal + 1) * band)
                    fresh = l == max(0, goal - 1)
                    if fresh:
                        target[:, where] = piece
                    else:
                        target[:, where] += piece

    def column(row):
        eye = lax.broadcasted_iota(jnp.int32, (CH, CH), 0) == lax.broadcasted_iota(jnp.int32, (CH, CH), 1)
        return jnp.sum(jnp.where(eye, row, 0.0), axis=1, keepdims=True)

    def line(col):
        eye = lax.broadcasted_iota(jnp.int32, (CH, CH), 0) == lax.broadcasted_iota(jnp.int32, (CH, CH), 1)
        return jnp.sum(jnp.where(eye, col, 0.0), axis=0, keepdims=True)

    gain = column(gain_ref[...])
    shift = column(shift_ref[...])
    eye_rows = KIN * FIELD_ROWS
    eye = jnp.where(
        lax.broadcasted_iota(jnp.int32, (eye_rows, eye_rows), 0)
        == lax.broadcasted_iota(jnp.int32, (eye_rows, eye_rows), 1),
        1.0,
        0.0,
    ).astype(BF16)

    flat[:, 0:LANES] = jnp.zeros((CH, LANES), F32)

    def first_pass(k):
        turned = nt(eye, batch_ref[k])
        blocks = [turned[b * FIELD_ROWS : b * FIELD_ROWS + 8] for b in range(KIN)]

        def store(where, value):
            sx[k, :, where] = value

        stack_taps(blocks, 1, store)
        mask = live(k)
        total = flat[:, 0:LANES]
        for l in range(PZ):
            got = mm(w1_ref[...], sx[k, :, l * band : (l + 1) * band])
            hidden[k, :, l * band : (l + 1) * band] = got
            for x in range(PX):
                total = total + got[:, x * LANES : (x + 1) * LANES] * mask
        flat[:, 0:LANES] = total

    each(chunks, first_pass)
    average = jnp.sum(flat[:, 0:LANES], axis=1, keepdims=True) / points
    flat[:, 0:LANES] = jnp.zeros((CH, LANES), F32)

    def second_pass(k):
        mask = live(k)
        total = flat[:, 0:LANES]
        for b in range(KIN):
            where = slice(b * LANES, (b + 1) * LANES)
            centred = hidden[k, :, where] - average
            hidden[k, :, where] = centred
            total = total + centred * centred * mask
        flat[:, 0:LANES] = total

    each(chunks, second_pass)
    variance = jnp.sum(flat[:, 0:LANES], axis=1, keepdims=True) / points
    inverse = lax.rsqrt(variance + EPSILON)

    g2[...] = jnp.zeros_like(g2)
    small[...] = jnp.zeros_like(small)
    flat[:, 0 : 2 * LANES] = jnp.zeros((CH, 2 * LANES), F32)
    flat[0:8, 2 * LANES : 3 * LANES] = jnp.zeros((8, LANES), F32)

    def main_pass(k):
        mask = live(k)

        def act_first(l, x):
            normed = hidden[k, :, at(l, x)] * inverse * gain + shift
            return normed * jax.nn.sigmoid(normed)

        stack_planes(act_first, 1)
        plane_products(w2f_ref, 1, h2)
        for b in range(KIN):
            where = slice(b * LANES, (b + 1) * LANES)
            pre = h2[:, where]
            act2[:, where] = (pre * jax.nn.sigmoid(pre)).astype(BF16)
        for l in range(PZ):
            where = slice(l * band, (l + 1) * band)
            tap_out[:, where] = mm(w3f_ref[...], act2[:, where])
        turned = nt(eye, batch_ref[k])
        errors = []
        lost = flat[0:8, 2 * LANES : 3 * LANES]
        for l in range(PZ):
            for x in range(PX):
                sums = {}
                for t, (dz, dx, dy) in enumerate(TAPS):
                    lz, xx = l + dz, x + dx
                    if 0 <= lz < PZ and 0 <= xx < PX:
                        piece = tap_out[t * 8 : (t + 1) * 8, at(lz, xx)]
                        sums[dy] = sums[dy] + piece if dy in sums else piece
                output = sums[0] + shifted(sums[-1], -1) + shifted(sums[1], 1)
                b = l * PX + x
                error = (output - turned[b * FIELD_ROWS + 8 : b * FIELD_ROWS + 16]) * mask
                lost = lost + error * error
                errors.append(2.0 * factor * error)
        flat[0:8, 2 * LANES : 3 * LANES] = lost

        def store(where, value):
            des[:, where] = value

        stack_taps(errors, -1, store)
        small[:, 0:CH] += nt(des[...], act2[...])
        for l in range(PZ):
            got = mm(w3b_ref[...], des[:, l * band : (l + 1) * band])
            for x in range(PX):
                where = at(l, x)
                cot = got[:, x * LANES : (x + 1) * LANES].astype(BF16).astype(F32)
                pre = h2[:, where]
                sig = jax.nn.sigmoid(pre)
                h2[:, where] = cot * (sig * (1.0 + pre * (1.0 - sig)))
        zero = jnp.zeros((CH, band), BF16)
        for l in range(PZ):
            piece = h2[:, l * band : (l + 1) * band].astype(BF16)
            for i, dz in enumerate(OFFSETS):
                if 0 <= l + dz < PZ:
                    dys[i * CH : (i + 1) * CH, (l + dz) * band : (l + dz + 1) * band] = piece
        dys[0:CH, (PZ - 1) * band :] = zero
        dys[2 * CH :, 0:band] = zero
        g2[...] += nt(dys[...], s2[...])
        stack_planes(lambda l, x: h2[:, at(l, x)], -1)
        plane_products(w2b_ref, -1, act_cot)
        by_gain = flat[:, 0:LANES]
        by_shift = flat[:, LANES : 2 * LANES]
        for b in range(KIN):
            where = slice(b * LANES, (b + 1) * LANES)
            cot = act_cot[:, where].astype(BF16).astype(F32)
            normal = hidden[k, :, where] * inverse
            normed = normal * gain + shift
            sig = jax.nn.sigmoid(normed)
            d_normed = cot * (sig * (1.0 + normed * (1.0 - sig)))
            by_gain = by_gain + d_normed * normal
            by_shift = by_shift + d_normed
            dn[k, :, where] = d_normed
        flat[:, 0:LANES] = by_gain
        flat[:, LANES : 2 * LANES] = by_shift

    act_cot = tap_out.at[0:CH]
    each(chunks, main_pass)
    grad_gain = jnp.sum(flat[:, 0:LANES], axis=1, keepdims=True)
    grad_shift = jnp.sum(flat[:, LANES : 2 * LANES], axis=1, keepdims=True)
    loss = jnp.sum(flat[0:8, 2 * LANES : 3 * LANES]) * factor

    from_mean = -inverse * (gain * grad_shift) / points
    from_variance = -(gain * grad_gain) * inverse * inverse / points
    scale = gain * inverse

    out_ref[...] = jnp.zeros_like(out_ref)

    def last_pass(k):
        mask = live(k)
        for b in range(KIN):
            where = slice(b * LANES, (b + 1) * LANES)
            d_hidden = dn[k, :, where] * scale + mask * (from_mean + from_variance * hidden[k, :, where])
            act2[:, where] = d_hidden.astype(BF16)
        small[:, CH:LANES] += nt(sx[k], act2[...])

    each(chunks, last_pass)

    for j in range(MID_TILES):
        out_ref[j * MID_ROWS : (j + 1) * MID_ROWS, :] = g2[:, j * LANES : (j + 1) * LANES]
    half = MID_ROWS // 2
    out_ref[HALF_BASE : HALF_BASE + half, 0:CH] = g2[0:half, MID_TILES * LANES :]
    out_ref[HALF_BASE : HALF_BASE + half, CH:LANES] = g2[half:, MID_TILES * LANES :]
    both = [small[pl.ds(o, 27, stride=8), :] for o in range(6)]
    planes = [pair[:, 0:CH] for pair in both] + [pair[:, CH:LANES] for pair in both[0:3]]
    for n, plane in enumerate(planes):
        base = PLANE_BASE + (n // 2) * PLANE_STEP
        side = (n % 2) * CH
        out_ref[base : base + 27, side : side + CH] = plane
    out_ref[MISC_BASE : MISC_BASE + 1, 0:CH] = line(grad_gain)
    out_ref[MISC_BASE : MISC_BASE + 1, CH:LANES] = line(grad_shift)
    out_ref[MISC_BASE + 1 : MISC_BASE + 2, :] = jnp.full((1, LANES), loss, F32)


def train(factor, count, batch, gain, shift, weights):
    chunks = batch.shape[0]
    width = KIN * LANES
    return pl.pallas_call(
        functools.partial(train_kernel, factor),
        out_shape=jax.ShapeDtypeStruct((EXCHANGE_ROWS, LANES), F32),
        in_specs=[SMEM] + [VMEM] * 8,
        out_specs=VMEM,
        scratch_shapes=[
            pltpu.VMEM((chunks, TAP_ROWS, width), BF16),
            pltpu.VMEM((chunks, CH, width), F32),
            pltpu.VMEM((9 * CH, width), BF16),
            pltpu.VMEM((CH, width), F32),
            pltpu.VMEM((CH, width), BF16),
            pltpu.VMEM((TAP_ROWS, width), F32),
            pltpu.VMEM((TAP_ROWS, width), BF16),
            pltpu.VMEM((3 * CH, width), BF16),
            pltpu.VMEM((chunks, CH, width), F32),
            pltpu.VMEM((CH, 3 * LANES), F32),
            pltpu.VMEM((3 * CH, 9 * CH), F32),
            pltpu.VMEM((TAP_ROWS, LANES), F32),
        ],
        compiler_params=PARAMS,
        name="train_step",
    )(count, batch, gain, shift, *weights)


def update_kernel(grad_ref, wf_ref, gain_ref, shift_ref, wm_ref, wl_ref, nf_ref, ng_ref, ns_ref, nm_ref, nl_ref):
    half = MID_ROWS // 2
    for z in range(3):
        for j in range(MID_TILES):
            block = grad_ref[j * MID_ROWS + z * CH : j * MID_ROWS + (z + 1) * CH, :]
            t = z * 9 + 2 * j
            nm_ref[t] = wm_ref[t] - LEARNING * block[:, :CH]
            nm_ref[t + 1] = wm_ref[t + 1] - LEARNING * block[:, CH:]
    fold = grad_ref[HALF_BASE : HALF_BASE + half, :]
    last = jnp.concatenate([fold[:, :CH], fold[:, CH:]], axis=0)
    for z in range(3):
        t = z * 9 + 8
        nm_ref[t] = wm_ref[t] - LEARNING * last[z * CH : (z + 1) * CH]
    for n in range(9):
        base = PLANE_BASE + (n // 2) * PLANE_STEP
        side = (n % 2) * CH
        plane = grad_ref[base : base + 27, side : side + CH]
        if n < 6:
            nl_ref[n] = wl_ref[n] - LEARNING * plane
        else:
            nf_ref[n - 6] = wf_ref[n - 6] - LEARNING * plane
    misc = grad_ref[MISC_BASE : MISC_BASE + 1, :]
    ng_ref[...] = gain_ref[...] - LEARNING * misc[:, :CH]
    ns_ref[...] = shift_ref[...] - LEARNING * misc[:, CH:]


def update(grads, wf, gain, shift, wm, wl):
    shapes = [wf, gain, shift, wm, wl]
    return pl.pallas_call(
        update_kernel,
        out_shape=tuple(jax.ShapeDtypeStruct(w.shape, F32) for w in shapes),
        in_specs=[VMEM] * 6,
        out_specs=(VMEM,) * 5,
        name="update",
    )(grads, *shapes)


def total(parts, axes):
    devices = lax.axis_size(axes)
    rows = parts.reshape(devices, EXCHANGE_ROWS // devices, LANES)
    mine = lax.all_to_all(rows, axes, split_axis=0, concat_axis=0, tiled=True)
    mine = jnp.sum(mine, axis=0)
    spread = jnp.broadcast_to(mine[None], rows.shape)
    whole = lax.all_to_all(spread, axes, split_axis=0, concat_axis=0, tiled=True)
    return whole.reshape(EXCHANGE_ROWS, LANES)


def on_device(
    velocity, crop_level, crop_x, crop_y, live_count, w_first, norm_gain, norm_shift, w_middle, w_last
):
    sources = lax.axis_size("sec")
    bands = lax.axis_size("band")
    assert bands == 2 and sources % 2 == 0
    groups = sources * bands
    sec = lax.axis_index("sec")
    odd = sec % 2
    band = lax.axis_index("band")
    place = jnp.stack([odd, band]).astype(jnp.int32)

    wf = jnp.transpose(w_first, (2, 0, 1))
    wl = jnp.transpose(w_last, (1, 0, 2))
    weights = arrange_weights(wf, w_middle, wl)

    head, tail = velocity[:, :, 0, :], velocity[:, :, -1, :]
    near = jnp.where(odd == 1, head, tail)
    far = jnp.where(odd == 1, tail, head)
    plane = jnp.where(band == 0, velocity[:, -1], velocity[:, 0])
    first = lax.ppermute(near, "sec", [(i, i ^ 1) for i in range(sources)])
    second = lax.ppermute(far, "sec", [(i, ((i + 1) ^ 1) - 1) for i in range(1, sources - 1)])
    beyond = lax.ppermute(plane, "band", [(0, 1), (1, 0)])

    velocity_next, crops = flow_step(
        place, crop_level.reshape(-1), crop_x.reshape(-1), crop_y.reshape(-1), velocity, first, second, beyond
    )
    crops = crops.reshape(sources, PY, KIN * FIELD_ROWS)
    batch = lax.all_to_all(crops, "sec", split_axis=0, concat_axis=0, tiled=True)
    batch = batch.reshape(sources // CHUNK, LANES, KIN * FIELD_ROWS)
    factor = 1.0 / (6.0 * PZ * PX * PY * (groups * sources * 5 // 8))
    gain, shift = norm_gain.reshape(1, CH), norm_shift.reshape(1, CH)
    parts = train(factor, live_count, batch, gain, shift, weights)
    grads = total(parts, ("sec", "band"))
    nf, ng, ns, nm, nl = update(grads, wf, gain, shift, w_middle, wl)
    return (
        velocity_next,
        jnp.transpose(nf, (1, 2, 0)),
        ng.reshape(CH),
        ns.reshape(CH),
        nm,
        jnp.transpose(nl, (1, 0, 2)),
        grads[MISC_BASE + 1, 0],
    )


def solution(mesh):
    in_specs = (
        P(None, "band", "sec", None),
        P("sec", "band", None),
        P("sec", "band", None),
        P("sec", "band", None),
        P(("sec", "band")),
        P(),
        P(),
        P(),
        P(),
        P(),
    )
    out_specs = (P(None, "band", "sec", None), P(), P(), P(), P(), P(), P())
    return jax.shard_map(
        on_device, mesh=mesh, in_specs=in_specs, out_specs=out_specs, check_vma=False
    )
```

```python
import functools

import jax
import jax.numpy as jnp
from jax import lax
from jax.experimental import pallas as pl
from jax.experimental.pallas import tpu as pltpu
from jax.sharding import PartitionSpec as P

PZ = 4
PX = 4
PY = 8
CH = 64
LANES = 128
KIN = PZ * PX
CHUNK = LANES // PY
FIELD_ROWS = 16
TAP_ROWS = 27 * 8

TIME_STEP = 0.2
VISCOSITY = 0.5
LEARNING = 1.0
EPSILON = 1e-05
PAIRS = ((0, 0), (1, 1), (2, 2), (0, 1), (0, 2), (1, 2))
OFFSETS = (-1, 0, 1)
TAPS = [(dz, dx, dy) for dz in OFFSETS for dx in OFFSETS for dy in OFFSETS]

F32 = jnp.float32
BF16 = jnp.bfloat16
VMEM = pl.BlockSpec(memory_space=pltpu.VMEM)
SMEM = pl.BlockSpec(memory_space=pltpu.SMEM)
HBM = pl.BlockSpec(memory_space=pltpu.HBM)


def small_params(mib):
    return pltpu.CompilerParams(vmem_limit_bytes=min(mib, 60) * 1024 * 1024)


MID_ROWS = 9 * CH
HALF_BASE = MID_ROWS
PLANE_BASE = HALF_BASE + MID_ROWS // 2
PLANE_STEP = 32
PLANE_ROWS = 5 * PLANE_STEP
MISC_BASE = PLANE_BASE + 4 * PLANE_STEP + 27


def nt(left, right):
    return lax.dot_general(left, right, (((1,), (1,)), ((), ())), preferred_element_type=F32)


def mm(left, right):
    return lax.dot_general(left, right, (((1,), (0,)), ((), ())), preferred_element_type=F32)


def tn(left, right):
    return lax.dot_general(left, right, (((0,), (0,)), ((), ())), preferred_element_type=F32)


def shares(devices):
    mid, rest = -(-PLANE_BASE // devices), -(-PLANE_ROWS // devices)
    top = -(-(mid + rest) // 8) * 8
    return mid, rest, top, top + -(-rest // 8) * 8


def padded_rows(devices):
    mid, rest, _, _ = shares(devices)
    return devices * mid, max(PLANE_BASE + PLANE_ROWS, devices * mid, PLANE_BASE + devices * rest)


def two_parts(value):
    high = value.astype(BF16)
    return high, (value - high.astype(F32)).astype(BF16)


def fill(value, rows):
    missing = rows - value.shape[0]
    return jnp.concatenate([value, jnp.zeros((missing, LANES), F32)], axis=0) if missing else value


def each(number, body):
    if number == 1:
        body(0)
    else:
        lax.fori_loop(0, number, lambda i, c: (body(i), c)[1], 0)


def weights_kernel(wf_ref, wm_ref, wl_ref, w1_ref, w2f_ref, w2b_ref, w3f_ref, w3b_ref, rows):
    rows[...] = jnp.zeros_like(rows)
    for c in range(3):
        rows[pl.ds(c, 27, stride=8), :] = wf_ref[c]
    w1_ref[...] = jnp.transpose(rows[...]).astype(BF16)
    rows[...] = jnp.zeros_like(rows)
    for o in range(6):
        rows[pl.ds(o, 27, stride=8), :] = wl_ref[o]
    w3f_ref[...] = rows[...].astype(BF16)
    w3b_ref[...] = jnp.transpose(rows[...]).astype(BF16)
    for zx in range(9):
        taps = [wm_ref[zx * 3 + i] for i in range(3)]
        rows_at = slice(zx * CH, (zx + 1) * CH)
        w2f_ref[rows_at, :] = jnp.concatenate(taps, axis=1).astype(BF16)
        w2b_ref[rows_at, :] = jnp.transpose(jnp.concatenate(taps, axis=0)).astype(BF16)


def arrange_weights(wf, wm, wl):
    return pl.pallas_call(
        weights_kernel,
        out_shape=(
            jax.ShapeDtypeStruct((CH, TAP_ROWS), BF16),
            jax.ShapeDtypeStruct((9 * CH, 3 * CH), BF16),
            jax.ShapeDtypeStruct((9 * CH, 3 * CH), BF16),
            jax.ShapeDtypeStruct((TAP_ROWS, CH), BF16),
            jax.ShapeDtypeStruct((CH, TAP_ROWS), BF16),
        ),
        in_specs=[VMEM] * 3,
        out_specs=(VMEM,) * 5,
        scratch_shapes=[pltpu.VMEM((TAP_ROWS, CH), F32)],
        compiler_params=small_params(6),
        name="arrange_weights",
    )(wf, wm, wl)


def lane_values(values_ref, which_row, base, lanes):
    which = (lanes % LANES) // PY
    out = jnp.zeros(lanes.shape, jnp.int32)
    for k in range(CHUNK):
        out = jnp.where(which == k, values_ref[which_row, 0, base + k], out)
    return out


def fold_parts(got, rows):
    return (got[0:rows] + got[rows : 2 * rows]) + got[2 * rows : 3 * rows]


def shift_down(items, offset, wanted):
    step = 1 << (len(items) - wanted).bit_length()
    while step > 1:
        step //= 2
        keep = min(len(items), wanted + step - 1)
        chosen = (offset & step) != 0
        items = [
            jnp.where(chosen, items[i + step], items[i]) if i + step < len(items) else items[i] for i in range(keep)
        ]
    return items


def x_window(cells, x_of):
    kept = cells[0 : 2 * PX]
    for o in range(1, cells.shape[0] // 2 - PX + 1):
        kept = jnp.where(x_of == o, cells[2 * o : 2 * o + 2 * PX], kept)
    return kept


def three_parts(value):
    high = value.astype(BF16)
    rest = value - high.astype(F32)
    middle = rest.astype(BF16)
    low = (rest - middle.astype(F32)).astype(BF16)
    return jnp.concatenate([high, middle, low], axis=0)


def edges_kernel(source_ref, v_ref, near_ref, far_ref, plane_ref, loads):
    odd = lax.axis_index("sec") % 2 == 1
    upper_band = lax.axis_index("band") == 1
    _, levels, nx, ny = v_ref.shape
    arrivals = [
        pltpu.make_async_copy(source_ref.at[:, l], v_ref.at[:, l], loads.at[l]) for l in range(levels)
    ]
    for arrival in arrivals:
        arrival.start()
    for arrival in arrivals:
        arrival.wait()
    for c in range(3):
        head = v_ref[c, :, 0, :]
        tail = v_ref[c, :, nx - 1, :]
        near_ref[c] = jnp.where(odd, head, tail)
        far_ref[c] = jnp.where(odd, tail, head)
        plane_ref[c] = jnp.where(upper_band, v_ref[c, 0], v_ref[c, levels - 1])


def in_hbm(array):
    return pltpu.with_memory_space_constraint(array, pltpu.HBM)


def edges_step(velocity):
    _, levels, nx, ny = velocity.shape
    side = jax.ShapeDtypeStruct((3, levels, ny), F32)
    return pl.pallas_call(
        edges_kernel,
        out_shape=(
            jax.ShapeDtypeStruct(velocity.shape, F32), side, side, jax.ShapeDtypeStruct((3, nx, ny), F32)
        ),
        in_specs=[HBM],
        out_specs=(VMEM,) * 4,
        scratch_shapes=[pltpu.SemaphoreType.DMA((levels,))],
        compiler_params=small_params(6),
        cost_estimate=cost(10**6, 3 * 10**6),
        name="edges_step",
    )(in_hbm(velocity))


def inner_kernel(
    level_ref, cx_ref, cy_ref, v_ref, vn_ref, cells_ref, picks_ref, goal_ref, where_ref, parts, chosen, spots, sems
):
    _, levels, nx, ny = v_ref.shape
    chunks = cells_ref.shape[0]
    arrivals = [
        pltpu.make_async_copy(ref, spots.at[n], sems.at[n]) for n, ref in enumerate((level_ref, cx_ref, cy_ref))
    ]
    for arrival in arrivals:
        arrival.start()
    row = lax.broadcasted_iota(jnp.int32, (nx, ny), 0)
    share, slope = TIME_STEP * VISCOSITY, TIME_STEP * 0.5
    for l in range(levels):
        centre = [v_ref[c, l] for c in range(3)]
        u, v, w = [slope * field for field in centre]
        to_east = jnp.where(row == nx - 1, 0.0, share - u)
        to_west = jnp.where(row == 0, 0.0, share + u)
        to_north, to_south = share - v, share + v
        to_upper, to_lower = share - w, share + w
        nxt = []
        for c in range(3):
            mid = centre[c]
            new = (1.0 - 6.0 * share) * mid
            new = new + to_east * pltpu.roll(mid, nx - 1, 0) + to_west * pltpu.roll(mid, 1, 0)
            new = new + to_north * pltpu.roll(mid, ny - 1, 1) + to_south * pltpu.roll(mid, 1, 1)
            if l + 1 < levels:
                new = new + to_upper * v_ref[c, l + 1]
            if l > 0:
                new = new + to_lower * v_ref[c, l - 1]
            vn_ref[c, l] = new
            nxt.append(new)
        parts[l * 9 * nx : (l + 1) * 9 * nx, :] = three_parts(jnp.concatenate(nxt, axis=0))

    lanes = lax.broadcasted_iota(jnp.int32, (1, 2 * LANES), 1)
    position = lax.broadcasted_iota(jnp.int32, (ny, 2 * LANES), 0)
    half = levels // 2
    span = half * 9 * nx
    for arrival in arrivals:
        arrival.wait()

    def chunk(k):
        level_of, x_of, y_of = [lane_values(spots, n, k * CHUNK, lanes) for n in range(3)]
        where_ref[k, 0:1] = level_of
        where_ref[k, 1:2] = x_of
        source = 2 * (y_of + lanes % PY) + lanes // LANES
        picks = jnp.where(position == source, 1.0, 0.0).astype(BF16)
        picks_ref[k] = picks
        for part in range(2):
            got = mm(parts[part * span : (part + 1) * span, :], picks)
            for i in range(half):
                at = i * 9 * nx
                chosen[part * half + i] = fold_parts(got[at : at + 9 * nx], 3 * nx)
        for c in range(3):
            take = slice(c * nx, (c + 1) * nx)
            kept = shift_down([chosen[l, take, :] for l in range(levels)], level_of, PZ)
            for l in range(PZ):
                cells_ref[k, l, c] = x_window(kept[l], x_of)

    each(chunks, chunk)
    ch_rows = 9 * PZ * 8
    r = lax.broadcasted_iota(jnp.int32, (ch_rows, KIN * FIELD_ROWS), 0)
    col = lax.broadcasted_iota(jnp.int32, (ch_rows, KIN * FIELD_ROWS), 1)
    channel = r >> 5
    slot = jnp.where(channel < 3, channel, channel + 5)
    goal = ((((r >> 3) & 3) * PX + ((r & 7) >> 1)) * FIELD_ROWS) + slot
    goal_ref[...] = jnp.where((col == goal) & ((r & 1) == 0), 1.0, 0.0).astype(BF16)


def beyond_terms(near_ref, far_ref, plane_ref, first_ref, second_ref, beyond_ref):
    odd = lax.axis_index("sec") % 2 == 1
    upper_band = lax.axis_index("band") == 1
    share = TIME_STEP * VISCOSITY
    slope = TIME_STEP * 0.5
    u_near, u_far, w_plane = near_ref[0], far_ref[0], plane_ref[2]
    at_west = share + slope * jnp.where(odd, u_near, u_far)
    at_east = share - slope * jnp.where(odd, u_far, u_near)
    at_plane = jnp.where(upper_band, share + slope * w_plane, share - slope * w_plane)
    west, east, plane = [], [], []
    for c in range(3):
        west.append(jnp.where(odd, first_ref[c], second_ref[c]) * at_west)
        east.append(jnp.where(odd, second_ref[c], first_ref[c]) * at_east)
        plane.append(beyond_ref[c] * at_plane)
    return upper_band, west, east, plane


def crop_kernel(
    where_ref, cells_ref, picks_ref, goal_ref, near_ref, far_ref, plane_ref, first_ref, second_ref, beyond_ref, crop_ref
):
    upper_band, west, east, plane = beyond_terms(near_ref, far_ref, plane_ref, first_ref, second_ref, beyond_ref)
    chunks = cells_ref.shape[0]
    levels, nx = west[0].shape[0], plane[0].shape[0]
    last_level, last_x = levels - PZ, nx // 2 - PX
    terms = three_parts(jnp.concatenate(west + east + plane, axis=0))
    lanes = lax.broadcasted_iota(jnp.int32, (1, 2 * LANES), 1)
    row = lax.broadcasted_iota(jnp.int32, (2 * PX, 2 * LANES), 0)

    def chunk(k):
        level_of = where_ref[k, 0:1]
        x_of = where_ref[k, 1:2]
        got = fold_parts(mm(terms, picks_ref[k]), 6 * levels + 3 * nx)
        window = [[None] * 3 for _ in range(PZ)]
        low_plane = upper_band & (level_of == 0)
        high_plane = jnp.logical_not(upper_band) & (level_of == last_level)
        for c in range(3):
            sides = []
            for side in (c, 3 + c):
                kept = got[side * levels : (side + 1) * levels]
                step = 1 << last_level.bit_length()
                while step > 1:
                    step //= 2
                    kept = jnp.where((level_of & step) != 0, pltpu.roll(kept, levels - step, 0), kept)
                sides.append(kept)
            at_west = jnp.where(x_of == 0, sides[0], 0.0)
            at_east = jnp.where(x_of == last_x, sides[1], 0.0)
            at_plane = x_window(got[6 * levels + c * nx : 6 * levels + (c + 1) * nx], x_of)
            for l in range(PZ):
                outer = jnp.where(row == 0, at_west[l : l + 1], 0.0) + jnp.where(
                    row == 2 * PX - 1, at_east[l : l + 1], 0.0
                )
                value = cells_ref[k, l, c] + outer
                if l == 0:
                    value = value + jnp.where(low_plane, at_plane, 0.0)
                if l == PZ - 1:
                    value = value + jnp.where(high_plane, at_plane, 0.0)
                window[l][c] = value

        def box(cells):
            pair = cells[:, :LANES] + cells[:, LANES:]
            return (pair + pltpu.roll(pair, 2 * PX - 1, 0)) * 0.25

        rows = [None] * (9 * PZ)
        for l in range(PZ):
            means = [box(cells) for cells in window[l]]
            for c in range(3):
                rows[c * PZ + l] = means[c]
            for n, (i, j) in enumerate(PAIRS):
                rows[(3 + n) * PZ + l] = box(window[l][i] * window[l][j]) - means[i] * means[j]
        fields = jnp.concatenate(rows, axis=0).astype(BF16)
        crop_ref[k] = tn(fields, goal_ref[...]).astype(BF16)

    each(chunks, chunk)


def finish_kernel(
    vn_ref, near_ref, far_ref, plane_ref, first_ref, second_ref, beyond_ref, out_ref, done, sems
):
    upper_band, west, east, plane = beyond_terms(near_ref, far_ref, plane_ref, first_ref, second_ref, beyond_ref)
    _, levels, nx, ny = vn_ref.shape
    row = lax.broadcasted_iota(jnp.int32, (nx, ny), 0)
    copies = []
    for l in range(levels):
        for c in range(3):
            value = vn_ref[c, l] + jnp.where(
                row == 0, west[c][l : l + 1], jnp.where(row == nx - 1, east[c][l : l + 1], 0.0)
            )
            if l == 0:
                value = value + jnp.where(upper_band, plane[c], 0.0)
            if l == levels - 1:
                value = value + jnp.where(upper_band, 0.0, plane[c])
            done[c, l] = value
        copy = pltpu.make_async_copy(done.at[:, l], out_ref.at[:, l], sems.at[l])
        copy.start()
        copies.append(copy)
    for copy in copies:
        copy.wait()


def cost(flops, moved):
    return pl.CostEstimate(flops=flops, bytes_accessed=moved, transcendentals=0)


def inner_step(level, cx, cy, velocity):
    samples = level.size
    chunks = samples // CHUNK
    _, levels, nx, ny = velocity.shape
    return pl.pallas_call(
        inner_kernel,
        out_shape=(
            jax.ShapeDtypeStruct(velocity.shape, F32),
            jax.ShapeDtypeStruct((chunks, PZ, 3, 2 * PX, 2 * LANES), F32),
            jax.ShapeDtypeStruct((chunks, ny, 2 * LANES), BF16),
            jax.ShapeDtypeStruct((9 * PZ * 8, KIN * FIELD_ROWS), BF16),
            jax.ShapeDtypeStruct((chunks, 8, 2 * LANES), jnp.int32),
        ),
        in_specs=[HBM, HBM, HBM, VMEM],
        out_specs=(VMEM,) * 5,
        scratch_shapes=[
            pltpu.VMEM((levels * 9 * nx, ny), BF16),
            pltpu.VMEM((levels, 3 * nx, 2 * LANES), F32),
            pltpu.SMEM((3, 1, samples), jnp.int32),
            pltpu.SemaphoreType.DMA((3,)),
        ],
        compiler_params=small_params(14 + 2 * chunks),
        cost_estimate=cost(3 * 10**9, 8 * 10**6),
        name="inner_step",
    )(*[in_hbm(x.reshape(1, samples)) for x in (level, cx, cy)], velocity)


def cut_crops(inner, edges):
    _, cells, picks, goal, where = inner
    chunks = cells.shape[0]
    return pl.pallas_call(
        crop_kernel,
        out_shape=jax.ShapeDtypeStruct((chunks, LANES, KIN * FIELD_ROWS), BF16),
        in_specs=[VMEM] * 10,
        out_specs=VMEM,
        compiler_params=small_params(6 + 2 * chunks),
        cost_estimate=cost(10**9, 3 * 10**6),
        name="cut_crops",
    )(where, cells, picks, goal, *edges)


def finish_step(inner, edges):
    vn = inner[0]
    return pl.pallas_call(
        finish_kernel,
        out_shape=jax.ShapeDtypeStruct(vn.shape, F32),
        in_specs=[VMEM] * 7,
        out_specs=HBM,
        scratch_shapes=[pltpu.VMEM(vn.shape, F32), pltpu.SemaphoreType.DMA((vn.shape[1],))],
        compiler_params=small_params(10),
        cost_estimate=cost(2 * 10**9, 4 * 10**6),
        name="finish_step",
    )(vn, *edges)


def train_kernel(
    factor, count_ref, batch_ref, gain_ref, shift_ref, w1_ref, w2f_ref, w2b_ref, w3f_ref, w3b_ref,
    packed_ref, sx, hidden, s2, h2, act2, tap_out, des, dys, dn, flat, g2, small, out_ref,
):
    chunks = batch_ref.shape[0]
    width = KIN * LANES
    band = PX * LANES
    count = count_ref[0]
    points = count.astype(F32) * (KIN * PY)
    lane = lax.broadcasted_iota(jnp.int32, (1, LANES), 1)
    y = lane % PY
    inside = {-1: y > 0, 1: y < PY - 1}

    def live(k):
        return jnp.where(k * CHUNK + lane // PY < count, 1.0, 0.0)

    def shifted(block, dy):
        if dy == 0:
            return block
        return jnp.where(inside[dy], pltpu.roll(block, (-dy) % LANES, 1), 0.0)

    def at(l, x):
        return slice((l * PX + x) * LANES, (l * PX + x + 1) * LANES)

    def stack_taps(blocks, sign, store):
        moved = {dy: [shifted(block, dy) for block in blocks] for dy in OFFSETS}
        zero = jnp.zeros((8, LANES), F32)
        for l in range(PZ):
            for x in range(PX):
                column = []
                for dz, dx, dy in TAPS:
                    lz, xx = l + sign * dz, x + sign * dx
                    ok = 0 <= lz < PZ and 0 <= xx < PX
                    column.append(moved[sign * dy][lz * PX + xx] if ok else zero)
                store(at(l, x), jnp.concatenate(column, axis=0).astype(BF16))

    def stack_rows(block_of, sign):
        for l in range(PZ):
            for x in range(PX):
                block = block_of(l, x)
                for i, dy in enumerate(OFFSETS):
                    s2[i * CH : (i + 1) * CH, at(l, x)] = shifted(block, sign * dy).astype(BF16)

    def plane_products(weights, sign, target):
        for l in range(PZ):
            got = mm(weights[...], s2[:, l * band : (l + 1) * band])
            for i, dz in enumerate(OFFSETS):
                goal = l - sign * dz
                if not 0 <= goal < PZ:
                    continue
                for x in range(PX):
                    piece = None
                    for j, dx in enumerate(OFFSETS):
                        source = x + sign * dx
                        if 0 <= source < PX:
                            n = i * 3 + j
                            term = got[n * CH : (n + 1) * CH, source * LANES : (source + 1) * LANES]
                            piece = term if piece is None else piece + term
                    if l == max(0, goal - 1):
                        target[:, at(goal, x)] = piece
                    else:
                        target[:, at(goal, x)] += piece

    def column(row):
        eye = lax.broadcasted_iota(jnp.int32, (CH, CH), 0) == lax.broadcasted_iota(jnp.int32, (CH, CH), 1)
        return jnp.sum(jnp.where(eye, row, 0.0), axis=1, keepdims=True)

    def line(col):
        eye = lax.broadcasted_iota(jnp.int32, (CH, CH), 0) == lax.broadcasted_iota(jnp.int32, (CH, CH), 1)
        return jnp.sum(jnp.where(eye, col, 0.0), axis=0, keepdims=True)

    gain = column(gain_ref[...])
    shift = column(shift_ref[...])
    eye_rows = KIN * FIELD_ROWS
    eye = jnp.where(
        lax.broadcasted_iota(jnp.int32, (eye_rows, eye_rows), 0)
        == lax.broadcasted_iota(jnp.int32, (eye_rows, eye_rows), 1),
        1.0,
        0.0,
    ).astype(BF16)

    flat[:, 0:LANES] = jnp.zeros((CH, LANES), F32)

    def first_pass(k):
        turned = nt(eye, batch_ref[k])
        blocks = [turned[b * FIELD_ROWS : b * FIELD_ROWS + 8] for b in range(KIN)]

        def store(where, value):
            sx[k, :, where] = value

        stack_taps(blocks, 1, store)
        mask = live(k)
        total = flat[:, 0:LANES]
        for l in range(PZ):
            got = mm(w1_ref[...], sx[k, :, l * band : (l + 1) * band])
            hidden[k, :, l * band : (l + 1) * band] = got
            for x in range(PX):
                total = total + got[:, x * LANES : (x + 1) * LANES] * mask
        flat[:, 0:LANES] = total

    each(chunks, first_pass)
    average = jnp.sum(flat[:, 0:LANES], axis=1, keepdims=True) / points
    flat[:, 0:LANES] = jnp.zeros((CH, LANES), F32)

    def second_pass(k):
        mask = live(k)
        total = flat[:, 0:LANES]
        for b in range(KIN):
            where = slice(b * LANES, (b + 1) * LANES)
            centred = hidden[k, :, where] - average
            hidden[k, :, where] = centred
            total = total + centred * centred * mask
        flat[:, 0:LANES] = total

    each(chunks, second_pass)
    variance = jnp.sum(flat[:, 0:LANES], axis=1, keepdims=True) / points
    inverse = lax.rsqrt(variance + EPSILON)

    g2[...] = jnp.zeros_like(g2)
    small[...] = jnp.zeros_like(small)
    flat[:, 0 : 2 * LANES] = jnp.zeros((CH, 2 * LANES), F32)
    flat[0:8, 2 * LANES : 3 * LANES] = jnp.zeros((8, LANES), F32)

    def main_pass(k):
        mask = live(k)

        def act_first(l, x):
            normed = hidden[k, :, at(l, x)] * inverse * gain + shift
            return normed * jax.nn.sigmoid(normed)

        stack_rows(act_first, 1)
        plane_products(w2f_ref, 1, h2)
        for b in range(KIN):
            where = slice(b * LANES, (b + 1) * LANES)
            pre = h2[:, where]
            act2[:, where] = (pre * jax.nn.sigmoid(pre)).astype(BF16)
        for l in range(PZ):
            where = slice(l * band, (l + 1) * band)
            tap_out[:, where] = mm(w3f_ref[...], act2[:, where])
        turned = nt(eye, batch_ref[k])
        errors = []
        lost = flat[0:8, 2 * LANES : 3 * LANES]
        for l in range(PZ):
            for x in range(PX):
                sums = {}
                for t, (dz, dx, dy) in enumerate(TAPS):
                    lz, xx = l + dz, x + dx
                    if 0 <= lz < PZ and 0 <= xx < PX:
                        piece = tap_out[t * 8 : (t + 1) * 8, at(lz, xx)]
                        sums[dy] = sums[dy] + piece if dy in sums else piece
                output = sums[0] + shifted(sums[-1], -1) + shifted(sums[1], 1)
                b = l * PX + x
                error = (output - turned[b * FIELD_ROWS + 8 : b * FIELD_ROWS + 16]) * mask
                lost = lost + error * error
                errors.append(2.0 * factor * error)
        flat[0:8, 2 * LANES : 3 * LANES] = lost

        def store(where, value):
            des[:, where] = value

        stack_taps(errors, -1, store)
        small[:, 0:CH] += nt(des[...], act2[...])
        for l in range(PZ):
            got = mm(w3b_ref[...], des[:, l * band : (l + 1) * band])
            for x in range(PX):
                where = at(l, x)
                cot = got[:, x * LANES : (x + 1) * LANES].astype(BF16).astype(F32)
                pre = h2[:, where]
                sig = jax.nn.sigmoid(pre)
                h2[:, where] = cot * (sig * (1.0 + pre * (1.0 - sig)))
        zero = jnp.zeros((CH, LANES), BF16)
        for l in range(PZ):
            for x in range(PX):
                piece = h2[:, at(l, x)].astype(BF16)
                for n in range(9):
                    goal, gx = l + n // 3 - 1, x + n % 3 - 1
                    if 0 <= goal < PZ and 0 <= gx < PX:
                        dys[n * CH : (n + 1) * CH, at(goal, gx)] = piece
                    source, sx_at = l - n // 3 + 1, x - n % 3 + 1
                    if not (0 <= source < PZ and 0 <= sx_at < PX):
                        dys[n * CH : (n + 1) * CH, at(l, x)] = zero
        g2[...] += nt(dys[...], s2[...])
        stack_rows(lambda l, x: h2[:, at(l, x)], -1)
        plane_products(w2b_ref, -1, act_cot)
        by_gain = flat[:, 0:LANES]
        by_shift = flat[:, LANES : 2 * LANES]
        for b in range(KIN):
            where = slice(b * LANES, (b + 1) * LANES)
            cot = act_cot[:, where].astype(BF16).astype(F32)
            normal = hidden[k, :, where] * inverse
            normed = normal * gain + shift
            sig = jax.nn.sigmoid(normed)
            d_normed = cot * (sig * (1.0 + normed * (1.0 - sig)))
            by_gain = by_gain + d_normed * normal
            by_shift = by_shift + d_normed
            dn[k, :, where] = d_normed
        flat[:, 0:LANES] = by_gain
        flat[:, LANES : 2 * LANES] = by_shift

    act_cot = tap_out.at[0:CH]
    each(chunks, main_pass)
    grad_gain = jnp.sum(flat[:, 0:LANES], axis=1, keepdims=True)
    grad_shift = jnp.sum(flat[:, LANES : 2 * LANES], axis=1, keepdims=True)
    loss = jnp.sum(flat[0:8, 2 * LANES : 3 * LANES]) * factor

    from_mean = -inverse * (gain * grad_shift) / points
    from_variance = -(gain * grad_gain) * inverse * inverse / points
    scale = gain * inverse

    out_ref[...] = jnp.zeros_like(out_ref)

    def last_pass(k):
        mask = live(k)
        for b in range(KIN):
            where = slice(b * LANES, (b + 1) * LANES)
            d_hidden = dn[k, :, where] * scale + mask * (from_mean + from_variance * hidden[k, :, where])
            act2[:, where] = d_hidden.astype(BF16)
        small[:, CH:LANES] += nt(sx[k], act2[...])

    each(chunks, last_pass)

    half = MID_ROWS // 2
    out_ref[0:MID_ROWS, :] = g2[:, 0:LANES]
    out_ref[HALF_BASE : HALF_BASE + half, 0:CH] = g2[0:half, LANES:]
    out_ref[HALF_BASE : HALF_BASE + half, CH:LANES] = g2[half:, LANES:]
    both = [small[pl.ds(o, 27, stride=8), :] for o in range(6)]
    planes = [pair[:, 0:CH] for pair in both] + [pair[:, CH:LANES] for pair in both[0:3]]
    for n, plane in enumerate(planes):
        base = PLANE_BASE + (n // 2) * PLANE_STEP
        side = (n % 2) * CH
        out_ref[base : base + 27, side : side + CH] = plane
    out_ref[MISC_BASE : MISC_BASE + 1, 0:CH] = line(grad_gain)
    out_ref[MISC_BASE : MISC_BASE + 1, CH:LANES] = line(grad_shift)
    out_ref[MISC_BASE + 1 : MISC_BASE + 2, :] = jnp.full((1, LANES), loss, F32)
    devices = packed_ref.shape[0]
    mid, rest, top, _ = shares(devices)
    for d in range(devices):
        own = out_ref[PLANE_BASE + d * rest : PLANE_BASE + (d + 1) * rest, :]
        high, low = two_parts(own)
        both = jnp.concatenate([out_ref[d * mid : (d + 1) * mid, :], own], axis=0)
        packed_ref[d, 0:top, :] = fill(both, top).astype(BF16)
        packed_ref[d, top:, :] = fill(low.astype(F32), packed_ref.shape[1] - top).astype(BF16)


def combine_kernel(parts_ref, out_ref):
    devices = parts_ref.shape[0]
    mid, rest, top, rows = shares(devices)
    total = parts_ref[0].astype(F32)
    for d in range(1, devices):
        total = total + parts_ref[d].astype(F32)
    own = total[mid : mid + rest] + total[top : top + rest]
    high, low = two_parts(own)
    whole = jnp.concatenate(
        [fill(jnp.concatenate([total[0:mid], own], axis=0), top), fill(low.astype(F32), rows - top)], axis=0
    ).astype(BF16)
    for d in range(devices):
        out_ref[d] = whole


def combine(parts):
    return pl.pallas_call(
        combine_kernel,
        out_shape=jax.ShapeDtypeStruct(parts.shape, BF16),
        in_specs=[VMEM],
        out_specs=VMEM,
        compiler_params=small_params(8),
        name="combine",
    )(parts)


def train(factor, devices, count, batch, gain, shift, weights):
    chunks = batch.shape[0]
    width = KIN * LANES
    return pl.pallas_call(
        functools.partial(train_kernel, factor),
        out_shape=jax.ShapeDtypeStruct((devices, shares(devices)[3], LANES), BF16),
        in_specs=[SMEM] + [VMEM] * 8,
        out_specs=VMEM,
        scratch_shapes=[
            pltpu.VMEM((chunks, TAP_ROWS, width), BF16),
            pltpu.VMEM((chunks, CH, width), F32),
            pltpu.VMEM((3 * CH, width), BF16),
            pltpu.VMEM((CH, width), F32),
            pltpu.VMEM((CH, width), BF16),
            pltpu.VMEM((TAP_ROWS, width), F32),
            pltpu.VMEM((TAP_ROWS, width), BF16),
            pltpu.VMEM((9 * CH, width), BF16),
            pltpu.VMEM((chunks, CH, width), F32),
            pltpu.VMEM((CH, 3 * LANES), F32),
            pltpu.VMEM((9 * CH, 3 * CH), F32),
            pltpu.VMEM((TAP_ROWS, LANES), F32),
            pltpu.VMEM((padded_rows(devices)[1], LANES), F32),
        ],
        compiler_params=small_params(20 + 4 * chunks),
        name="train_step",
    )(count, batch, gain, shift, *weights)


def update_kernel(
    whole_ref, wf_ref, gain_ref, shift_ref, wm_ref, wl_ref, nf_ref, ng_ref, ns_ref, nm_ref, nl_ref, loss_ref, grad_ref
):
    devices = whole_ref.shape[0]
    mid, rest, top, _ = shares(devices)
    for d in range(devices):
        grad_ref[d * mid : (d + 1) * mid, :] = whole_ref[d, 0:top, :].astype(F32)[0:mid]
    for d in range(devices):
        high = whole_ref[d, 0:top, :].astype(F32)[mid : mid + rest]
        low = whole_ref[d, top:, :].astype(F32)[0:rest]
        grad_ref[PLANE_BASE + d * rest : PLANE_BASE + (d + 1) * rest, :] = high + low
    half = MID_ROWS // 2
    fold = grad_ref[HALF_BASE : HALF_BASE + half, :]
    last = jnp.concatenate([fold[:, :CH], fold[:, CH:]], axis=0)
    for zx in range(9):
        rows_at = slice(zx * CH, (zx + 1) * CH)
        block = grad_ref[rows_at, :]
        nm_ref[zx * 3] = wm_ref[zx * 3] - LEARNING * block[:, :CH]
        nm_ref[zx * 3 + 1] = wm_ref[zx * 3 + 1] - LEARNING * block[:, CH:]
        nm_ref[zx * 3 + 2] = wm_ref[zx * 3 + 2] - LEARNING * last[rows_at]
    for n in range(9):
        base = PLANE_BASE + (n // 2) * PLANE_STEP
        side = (n % 2) * CH
        plane = grad_ref[base : base + 27, side : side + CH]
        if n < 6:
            nl_ref[n] = wl_ref[n] - LEARNING * plane
        else:
            nf_ref[n - 6] = wf_ref[n - 6] - LEARNING * plane
    misc = grad_ref[MISC_BASE : MISC_BASE + 1, :]
    ng_ref[...] = gain_ref[...] - LEARNING * misc[:, :CH]
    ns_ref[...] = shift_ref[...] - LEARNING * misc[:, CH:]
    loss_ref[...] = grad_ref[MISC_BASE + 1 : MISC_BASE + 2, 0:1]


def update(whole, wf, gain, shift, wm, wl):
    shapes = [wf, gain, shift, wm, wl]
    return pl.pallas_call(
        update_kernel,
        out_shape=tuple(jax.ShapeDtypeStruct(w.shape, F32) for w in shapes) + (jax.ShapeDtypeStruct((1, 1), F32),),
        in_specs=[VMEM] * 6,
        out_specs=(VMEM,) * 6,
        scratch_shapes=[pltpu.VMEM((padded_rows(whole.shape[0])[1], LANES), F32)],
        compiler_params=small_params(12),
        name="update",
    )(whole, *shapes)


def exchange(rows):
    return lax.all_to_all(rows, ("sec", "band"), split_axis=0, concat_axis=0, tiled=True)


def on_device(
    velocity, crop_level, crop_x, crop_y, live_count, w_first, norm_gain, norm_shift, w_middle, w_last
):
    sources = lax.axis_size("sec")
    bands = lax.axis_size("band")
    assert bands == 2 and sources % 2 == 0
    groups = sources * bands
    wf = jnp.transpose(w_first, (2, 0, 1))
    wl = jnp.transpose(w_last, (1, 0, 2))
    weights = arrange_weights(wf, w_middle, wl)

    held, near, far, plane = edges_step(velocity)
    first = lax.ppermute(near, "sec", [(i, i ^ 1) for i in range(sources)])
    second = lax.ppermute(far, "sec", [(i, ((i + 1) ^ 1) - 1) for i in range(1, sources - 1)])
    beyond = lax.ppermute(plane, "band", [(0, 1), (1, 0)])

    inner = inner_step(crop_level, crop_x, crop_y, held)
    edges = (near, far, plane, first, second, beyond)
    crops = cut_crops(inner, edges)
    velocity_next = finish_step(inner, edges)
    crops = crops.reshape(sources, PY, KIN * FIELD_ROWS)
    batch = lax.all_to_all(crops, "sec", split_axis=0, concat_axis=0, tiled=True)
    batch, velocity_next = lax.optimization_barrier((batch, velocity_next))
    batch = batch.reshape(sources // CHUNK, LANES, KIN * FIELD_ROWS)
    factor = 1.0 / (6.0 * PZ * PX * PY * (groups * sources * 5 // 8))
    gain, shift = norm_gain.reshape(1, CH), norm_shift.reshape(1, CH)
    parts = train(factor, groups, live_count, batch, gain, shift, weights)
    whole = exchange(combine(exchange(parts)))
    nf, ng, ns, nm, nl, loss = update(whole, wf, gain, shift, w_middle, wl)
    return (
        velocity_next,
        jnp.transpose(nf, (1, 2, 0)),
        ng.reshape(CH),
        ns.reshape(CH),
        nm,
        jnp.transpose(nl, (1, 0, 2)),
        loss.reshape(()),
    )


def solution(mesh):
    in_specs = (
        P(None, "band", "sec", None),
        P("sec", "band", None),
        P("sec", "band", None),
        P("sec", "band", None),
        P(("sec", "band")),
        P(),
        P(),
        P(),
        P(),
        P(),
    )
    out_specs = (P(None, "band", "sec", None), P(), P(), P(), P(), P(), P())
    return jax.shard_map(
        on_device, mesh=mesh, in_specs=in_specs, out_specs=out_specs, check_vma=False
    )
```

```python
import functools

import jax
import jax.numpy as jnp
from jax import lax
from jax.experimental import pallas as pl
from jax.experimental.pallas import tpu as pltpu
from jax.sharding import PartitionSpec as P

PZ = 4
PX = 4
PY = 8
CH = 64
LANES = 128
KIN = PZ * PX
CHUNK = LANES // PY
FIELD_ROWS = 16
TAP_ROWS = 27 * 8

TIME_STEP = 0.2
VISCOSITY = 0.5
LEARNING = 1.0
EPSILON = 1e-05
PAIRS = ((0, 0), (1, 1), (2, 2), (0, 1), (0, 2), (1, 2))
OFFSETS = (-1, 0, 1)
TAPS = [(dz, dx, dy) for dz in OFFSETS for dx in OFFSETS for dy in OFFSETS]

F32 = jnp.float32
BF16 = jnp.bfloat16
VMEM = pl.BlockSpec(memory_space=pltpu.VMEM)
SMEM = pl.BlockSpec(memory_space=pltpu.SMEM)
HBM = pl.BlockSpec(memory_space=pltpu.HBM)


def small_params(mib):
    return pltpu.CompilerParams(vmem_limit_bytes=min(mib, 60) * 1024 * 1024)


MID_ROWS = 9 * CH
HALF_BASE = MID_ROWS
PLANE_BASE = HALF_BASE + MID_ROWS // 2
PLANE_STEP = 32
PLANE_ROWS = 5 * PLANE_STEP
MISC_BASE = PLANE_BASE + 4 * PLANE_STEP + 27


def nt(left, right):
    return lax.dot_general(left, right, (((1,), (1,)), ((), ())), preferred_element_type=F32)


def mm(left, right):
    return lax.dot_general(left, right, (((1,), (0,)), ((), ())), preferred_element_type=F32)


def tn(left, right):
    return lax.dot_general(left, right, (((0,), (0,)), ((), ())), preferred_element_type=F32)


def shares(devices):
    mid, rest = -(-PLANE_BASE // devices), -(-PLANE_ROWS // devices)
    top = -(-(mid + rest) // 8) * 8
    return mid, rest, top, top + -(-rest // 8) * 8


def padded_rows(devices):
    mid, rest, _, _ = shares(devices)
    return devices * mid, max(PLANE_BASE + PLANE_ROWS, devices * mid, PLANE_BASE + devices * rest)


def two_parts(value):
    high = value.astype(BF16)
    return high, (value - high.astype(F32)).astype(BF16)


def fill(value, rows):
    missing = rows - value.shape[0]
    return jnp.concatenate([value, jnp.zeros((missing, LANES), F32)], axis=0) if missing else value


def each(number, body):
    if number == 1:
        body(0)
    else:
        lax.fori_loop(0, number, lambda i, c: (body(i), c)[1], 0)


def weights_kernel(wf_ref, wm_ref, wl_ref, w1_ref, w2f_ref, w2b_ref, w3f_ref, w3b_ref, rows):
    rows[...] = jnp.zeros_like(rows)
    for c in range(3):
        rows[pl.ds(c, 27, stride=8), :] = wf_ref[c]
    w1_ref[...] = jnp.transpose(rows[...]).astype(BF16)
    rows[...] = jnp.zeros_like(rows)
    for o in range(6):
        rows[pl.ds(o, 27, stride=8), :] = wl_ref[o]
    w3f_ref[...] = rows[...].astype(BF16)
    w3b_ref[...] = jnp.transpose(rows[...]).astype(BF16)
    for zx in range(9):
        taps = [wm_ref[zx * 3 + i] for i in range(3)]
        rows_at = slice(zx * CH, (zx + 1) * CH)
        w2f_ref[rows_at, :] = jnp.concatenate(taps, axis=1).astype(BF16)
        w2b_ref[rows_at, :] = jnp.transpose(jnp.concatenate(taps, axis=0)).astype(BF16)


def arrange_weights(wf, wm, wl):
    return pl.pallas_call(
        weights_kernel,
        out_shape=(
            jax.ShapeDtypeStruct((CH, TAP_ROWS), BF16),
            jax.ShapeDtypeStruct((9 * CH, 3 * CH), BF16),
            jax.ShapeDtypeStruct((9 * CH, 3 * CH), BF16),
            jax.ShapeDtypeStruct((TAP_ROWS, CH), BF16),
            jax.ShapeDtypeStruct((CH, TAP_ROWS), BF16),
        ),
        in_specs=[VMEM] * 3,
        out_specs=(VMEM,) * 5,
        scratch_shapes=[pltpu.VMEM((TAP_ROWS, CH), F32)],
        compiler_params=small_params(6),
        name="arrange_weights",
    )(wf, wm, wl)


def lane_values(values_ref, which_row, base, lanes):
    which = (lanes % LANES) // PY
    out = jnp.zeros(lanes.shape, jnp.int32)
    for k in range(CHUNK):
        out = jnp.where(which == k, values_ref[which_row, 0, base + k], out)
    return out


def fold_parts(got, rows):
    return (got[0:rows] + got[rows : 2 * rows]) + got[2 * rows : 3 * rows]


def shift_down(items, offset, wanted):
    step = 1 << (len(items) - wanted).bit_length()
    while step > 1:
        step //= 2
        keep = min(len(items), wanted + step - 1)
        chosen = (offset & step) != 0
        items = [
            jnp.where(chosen, items[i + step], items[i]) if i + step < len(items) else items[i] for i in range(keep)
        ]
    return items


def x_window(cells, x_of):
    kept = cells[0 : 2 * PX]
    for o in range(1, cells.shape[0] // 2 - PX + 1):
        kept = jnp.where(x_of == o, cells[2 * o : 2 * o + 2 * PX], kept)
    return kept


def three_parts(value):
    high = value.astype(BF16)
    rest = value - high.astype(F32)
    middle = rest.astype(BF16)
    low = (rest - middle.astype(F32)).astype(BF16)
    return jnp.concatenate([high, middle, low], axis=0)


def edges_kernel(source_ref, v_ref, near_ref, far_ref, plane_ref, loads):
    odd = lax.axis_index("sec") % 2 == 1
    upper_band = lax.axis_index("band") == 1
    _, levels, nx, ny = v_ref.shape
    arrivals = [
        pltpu.make_async_copy(source_ref.at[:, l], v_ref.at[:, l], loads.at[l]) for l in range(levels)
    ]
    for arrival in arrivals:
        arrival.start()
    for arrival in arrivals:
        arrival.wait()
    for c in range(3):
        head = v_ref[c, :, 0, :]
        tail = v_ref[c, :, nx - 1, :]
        near_ref[c] = jnp.where(odd, head, tail)
        far_ref[c] = jnp.where(odd, tail, head)
        plane_ref[c] = jnp.where(upper_band, v_ref[c, 0], v_ref[c, levels - 1])


def in_hbm(array):
    return pltpu.with_memory_space_constraint(array, pltpu.HBM)


def edges_step(velocity):
    _, levels, nx, ny = velocity.shape
    side = jax.ShapeDtypeStruct((3, levels, ny), F32)
    return pl.pallas_call(
        edges_kernel,
        out_shape=(
            jax.ShapeDtypeStruct(velocity.shape, F32), side, side, jax.ShapeDtypeStruct((3, nx, ny), F32)
        ),
        in_specs=[HBM],
        out_specs=(VMEM,) * 4,
        scratch_shapes=[pltpu.SemaphoreType.DMA((levels,))],
        compiler_params=small_params(6),
        cost_estimate=cost(10**6, 3 * 10**6),
        name="edges_step",
    )(in_hbm(velocity))


def inner_kernel(
    level_ref, cx_ref, cy_ref, v_ref, vn_ref, cells_ref, picks_ref, goal_ref, where_ref, parts, chosen, spots, sems
):
    _, levels, nx, ny = v_ref.shape
    chunks = cells_ref.shape[0]
    arrivals = [
        pltpu.make_async_copy(ref, spots.at[n], sems.at[n]) for n, ref in enumerate((level_ref, cx_ref, cy_ref))
    ]
    for arrival in arrivals:
        arrival.start()
    row = lax.broadcasted_iota(jnp.int32, (nx, ny), 0)
    share, slope = TIME_STEP * VISCOSITY, TIME_STEP * 0.5
    for l in range(levels):
        centre = [v_ref[c, l] for c in range(3)]
        u, v, w = [slope * field for field in centre]
        to_east = jnp.where(row == nx - 1, 0.0, share - u)
        to_west = jnp.where(row == 0, 0.0, share + u)
        to_north, to_south = share - v, share + v
        to_upper, to_lower = share - w, share + w
        nxt = []
        for c in range(3):
            mid = centre[c]
            new = (1.0 - 6.0 * share) * mid
            new = new + to_east * pltpu.roll(mid, nx - 1, 0) + to_west * pltpu.roll(mid, 1, 0)
            new = new + to_north * pltpu.roll(mid, ny - 1, 1) + to_south * pltpu.roll(mid, 1, 1)
            if l + 1 < levels:
                new = new + to_upper * v_ref[c, l + 1]
            if l > 0:
                new = new + to_lower * v_ref[c, l - 1]
            vn_ref[c, l] = new
            nxt.append(new)
        parts[l * 9 * nx : (l + 1) * 9 * nx, :] = three_parts(jnp.concatenate(nxt, axis=0))

    lanes = lax.broadcasted_iota(jnp.int32, (1, 2 * LANES), 1)
    position = lax.broadcasted_iota(jnp.int32, (ny, 2 * LANES), 0)
    half = levels // 2
    span = half * 9 * nx
    for arrival in arrivals:
        arrival.wait()

    def chunk(k):
        level_of, x_of, y_of = [lane_values(spots, n, k * CHUNK, lanes) for n in range(3)]
        where_ref[k, 0:1] = level_of
        where_ref[k, 1:2] = x_of
        source = 2 * (y_of + lanes % PY) + lanes // LANES
        picks = jnp.where(position == source, 1.0, 0.0).astype(BF16)
        picks_ref[k] = picks
        for part in range(2):
            got = mm(parts[part * span : (part + 1) * span, :], picks)
            for i in range(half):
                at = i * 9 * nx
                chosen[part * half + i] = fold_parts(got[at : at + 9 * nx], 3 * nx)
        for c in range(3):
            take = slice(c * nx, (c + 1) * nx)
            kept = shift_down([chosen[l, take, :] for l in range(levels)], level_of, PZ)
            for l in range(PZ):
                cells_ref[k, l, c] = x_window(kept[l], x_of)

    each(chunks, chunk)
    ch_rows = 9 * PZ * 8
    r = lax.broadcasted_iota(jnp.int32, (ch_rows, KIN * FIELD_ROWS), 0)
    col = lax.broadcasted_iota(jnp.int32, (ch_rows, KIN * FIELD_ROWS), 1)
    channel = r >> 5
    slot = jnp.where(channel < 3, channel, channel + 5)
    goal = ((((r >> 3) & 3) * PX + ((r & 7) >> 1)) * FIELD_ROWS) + slot
    goal_ref[...] = jnp.where((col == goal) & ((r & 1) == 0), 1.0, 0.0).astype(BF16)


def beyond_terms(near_ref, far_ref, plane_ref, first_ref, second_ref, beyond_ref):
    odd = lax.axis_index("sec") % 2 == 1
    upper_band = lax.axis_index("band") == 1
    share = TIME_STEP * VISCOSITY
    slope = TIME_STEP * 0.5
    u_near, u_far, w_plane = near_ref[0], far_ref[0], plane_ref[2]
    at_west = share + slope * jnp.where(odd, u_near, u_far)
    at_east = share - slope * jnp.where(odd, u_far, u_near)
    at_plane = jnp.where(upper_band, share + slope * w_plane, share - slope * w_plane)
    west, east, plane = [], [], []
    for c in range(3):
        west.append(jnp.where(odd, first_ref[c], second_ref[c]) * at_west)
        east.append(jnp.where(odd, second_ref[c], first_ref[c]) * at_east)
        plane.append(beyond_ref[c] * at_plane)
    return upper_band, west, east, plane


def crop_kernel(
    where_ref, cells_ref, picks_ref, goal_ref, near_ref, far_ref, plane_ref, first_ref, second_ref, beyond_ref, crop_ref
):
    upper_band, west, east, plane = beyond_terms(near_ref, far_ref, plane_ref, first_ref, second_ref, beyond_ref)
    chunks = cells_ref.shape[0]
    levels, nx = west[0].shape[0], plane[0].shape[0]
    last_level, last_x = levels - PZ, nx // 2 - PX
    terms = three_parts(jnp.concatenate(west + east + plane, axis=0))
    lanes = lax.broadcasted_iota(jnp.int32, (1, 2 * LANES), 1)
    row = lax.broadcasted_iota(jnp.int32, (2 * PX, 2 * LANES), 0)

    def chunk(k):
        level_of = where_ref[k, 0:1]
        x_of = where_ref[k, 1:2]
        got = fold_parts(mm(terms, picks_ref[k]), 6 * levels + 3 * nx)
        window = [[None] * 3 for _ in range(PZ)]
        low_plane = upper_band & (level_of == 0)
        high_plane = jnp.logical_not(upper_band) & (level_of == last_level)
        for c in range(3):
            sides = []
            for side in (c, 3 + c):
                kept = got[side * levels : (side + 1) * levels]
                step = 1 << last_level.bit_length()
                while step > 1:
                    step //= 2
                    kept = jnp.where((level_of & step) != 0, pltpu.roll(kept, levels - step, 0), kept)
                sides.append(kept)
            at_west = jnp.where(x_of == 0, sides[0], 0.0)
            at_east = jnp.where(x_of == last_x, sides[1], 0.0)
            at_plane = x_window(got[6 * levels + c * nx : 6 * levels + (c + 1) * nx], x_of)
            for l in range(PZ):
                outer = jnp.where(row == 0, at_west[l : l + 1], 0.0) + jnp.where(
                    row == 2 * PX - 1, at_east[l : l + 1], 0.0
                )
                value = cells_ref[k, l, c] + outer
                if l == 0:
                    value = value + jnp.where(low_plane, at_plane, 0.0)
                if l == PZ - 1:
                    value = value + jnp.where(high_plane, at_plane, 0.0)
                window[l][c] = value

        def box(cells):
            pair = cells[:, :LANES] + cells[:, LANES:]
            return (pair + pltpu.roll(pair, 2 * PX - 1, 0)) * 0.25

        rows = [None] * (9 * PZ)
        for l in range(PZ):
            means = [box(cells) for cells in window[l]]
            for c in range(3):
                rows[c * PZ + l] = means[c]
            for n, (i, j) in enumerate(PAIRS):
                rows[(3 + n) * PZ + l] = box(window[l][i] * window[l][j]) - means[i] * means[j]
        fields = jnp.concatenate(rows, axis=0).astype(BF16)
        crop_ref[k] = tn(fields, goal_ref[...]).astype(BF16)

    each(chunks, chunk)


def finish_kernel(
    vn_ref, near_ref, far_ref, plane_ref, first_ref, second_ref, beyond_ref, out_ref, done, sems
):
    upper_band, west, east, plane = beyond_terms(near_ref, far_ref, plane_ref, first_ref, second_ref, beyond_ref)
    _, levels, nx, ny = vn_ref.shape
    row = lax.broadcasted_iota(jnp.int32, (nx, ny), 0)
    copies = []
    for l in range(levels):
        for c in range(3):
            value = vn_ref[c, l] + jnp.where(
                row == 0, west[c][l : l + 1], jnp.where(row == nx - 1, east[c][l : l + 1], 0.0)
            )
            if l == 0:
                value = value + jnp.where(upper_band, plane[c], 0.0)
            if l == levels - 1:
                value = value + jnp.where(upper_band, 0.0, plane[c])
            done[c, l] = value
        copy = pltpu.make_async_copy(done.at[:, l], out_ref.at[:, l], sems.at[l])
        copy.start()
        copies.append(copy)
    for copy in copies:
        copy.wait()


def cost(flops, moved):
    return pl.CostEstimate(flops=flops, bytes_accessed=moved, transcendentals=0)


def inner_step(level, cx, cy, velocity):
    samples = level.size
    chunks = samples // CHUNK
    _, levels, nx, ny = velocity.shape
    return pl.pallas_call(
        inner_kernel,
        out_shape=(
            jax.ShapeDtypeStruct(velocity.shape, F32),
            jax.ShapeDtypeStruct((chunks, PZ, 3, 2 * PX, 2 * LANES), F32),
            jax.ShapeDtypeStruct((chunks, ny, 2 * LANES), BF16),
            jax.ShapeDtypeStruct((9 * PZ * 8, KIN * FIELD_ROWS), BF16),
            jax.ShapeDtypeStruct((chunks, 8, 2 * LANES), jnp.int32),
        ),
        in_specs=[HBM, HBM, HBM, VMEM],
        out_specs=(VMEM,) * 5,
        scratch_shapes=[
            pltpu.VMEM((levels * 9 * nx, ny), BF16),
            pltpu.VMEM((levels, 3 * nx, 2 * LANES), F32),
            pltpu.SMEM((3, 1, samples), jnp.int32),
            pltpu.SemaphoreType.DMA((3,)),
        ],
        compiler_params=small_params(14 + 2 * chunks),
        cost_estimate=cost(3 * 10**9, 8 * 10**6),
        name="inner_step",
    )(*[in_hbm(x.reshape(1, samples)) for x in (level, cx, cy)], velocity)


def cut_crops(inner, edges):
    _, cells, picks, goal, where = inner
    chunks = cells.shape[0]
    return pl.pallas_call(
        crop_kernel,
        out_shape=jax.ShapeDtypeStruct((chunks, LANES, KIN * FIELD_ROWS), BF16),
        in_specs=[VMEM] * 10,
        out_specs=VMEM,
        compiler_params=small_params(6 + 2 * chunks),
        cost_estimate=cost(10**9, 3 * 10**6),
        name="cut_crops",
    )(where, cells, picks, goal, *edges)


def finish_step(inner, edges):
    vn = inner[0]
    return pl.pallas_call(
        finish_kernel,
        out_shape=jax.ShapeDtypeStruct(vn.shape, F32),
        in_specs=[VMEM] * 7,
        out_specs=HBM,
        scratch_shapes=[pltpu.VMEM(vn.shape, F32), pltpu.SemaphoreType.DMA((vn.shape[1],))],
        compiler_params=small_params(10),
        cost_estimate=cost(2 * 10**9, 4 * 10**6),
        name="finish_step",
    )(vn, *edges)


def train_kernel(
    factor, count_ref, batch_ref, gain_ref, shift_ref, w1_ref, w2f_ref, w2b_ref, w3f_ref, w3b_ref,
    mine_ref, theirs_ref, sx, hidden, s2, s3, h2, act2, tap_out, des, dys, dn, flat, g2, small, out_ref,
):
    chunks = batch_ref.shape[0]
    width = KIN * LANES
    band = PX * LANES
    count = count_ref[0]
    points = count.astype(F32) * (KIN * PY)
    lane = lax.broadcasted_iota(jnp.int32, (1, LANES), 1)
    y = lane % PY
    inside = {-1: y > 0, 1: y < PY - 1}

    def live(k):
        return jnp.where(k * CHUNK + lane // PY < count, 1.0, 0.0)

    def shifted(block, dy):
        if dy == 0:
            return block
        return jnp.where(inside[dy], pltpu.roll(block, (-dy) % LANES, 1), 0.0)

    def at(l, x):
        return slice((l * PX + x) * LANES, (l * PX + x + 1) * LANES)

    def stack_taps(blocks, sign, store):
        moved = {dy: [shifted(block, dy) for block in blocks] for dy in OFFSETS}
        zero = jnp.zeros((8, LANES), F32)
        for l in range(PZ):
            for x in range(PX):
                column = []
                for dz, dx, dy in TAPS:
                    lz, xx = l + sign * dz, x + sign * dx
                    ok = 0 <= lz < PZ and 0 <= xx < PX
                    column.append(moved[sign * dy][lz * PX + xx] if ok else zero)
                store(at(l, x), jnp.concatenate(column, axis=0).astype(BF16))

    def stack_rows(block_of, sign, stack):
        for l in range(PZ):
            for x in range(PX):
                block = block_of(l, x)
                for i, dy in enumerate(OFFSETS):
                    stack[i * CH : (i + 1) * CH, at(l, x)] = shifted(block, sign * dy).astype(BF16)

    def plane_products(weights, stack, sign, target):
        for l in range(PZ):
            got = mm(weights[...], stack[:, l * band : (l + 1) * band])
            for i, dz in enumerate(OFFSETS):
                goal = l - sign * dz
                if not 0 <= goal < PZ:
                    continue
                for x in range(PX):
                    piece = None
                    for j, dx in enumerate(OFFSETS):
                        source = x + sign * dx
                        if 0 <= source < PX:
                            n = i * 3 + j
                            term = got[n * CH : (n + 1) * CH, source * LANES : (source + 1) * LANES]
                            piece = term if piece is None else piece + term
                    if l == max(0, goal - 1):
                        target[:, at(goal, x)] = piece
                    else:
                        target[:, at(goal, x)] += piece

    def add_to(ref, columns, value):
        if chunks > 1:
            ref[:, columns] += value
        else:
            ref[:, columns] = value

    def column(row):
        eye = lax.broadcasted_iota(jnp.int32, (CH, CH), 0) == lax.broadcasted_iota(jnp.int32, (CH, CH), 1)
        return jnp.sum(jnp.where(eye, row, 0.0), axis=1, keepdims=True)

    def line(col):
        eye = lax.broadcasted_iota(jnp.int32, (CH, CH), 0) == lax.broadcasted_iota(jnp.int32, (CH, CH), 1)
        return jnp.sum(jnp.where(eye, col, 0.0), axis=0, keepdims=True)

    gain = column(gain_ref[...])
    shift = column(shift_ref[...])
    eye_rows = KIN * FIELD_ROWS
    eye = jnp.where(
        lax.broadcasted_iota(jnp.int32, (eye_rows, eye_rows), 0)
        == lax.broadcasted_iota(jnp.int32, (eye_rows, eye_rows), 1),
        1.0,
        0.0,
    ).astype(BF16)

    flat[:, 0:LANES] = jnp.zeros((CH, LANES), F32)

    def first_pass(k):
        turned = nt(eye, batch_ref[k])
        blocks = [turned[b * FIELD_ROWS : b * FIELD_ROWS + 8] for b in range(KIN)]

        def store(where, value):
            sx[k, :, where] = value

        stack_taps(blocks, 1, store)
        mask = live(k)
        total = flat[:, 0:LANES]
        for l in range(PZ):
            got = mm(w1_ref[...], sx[k, :, l * band : (l + 1) * band])
            hidden[k, :, l * band : (l + 1) * band] = got
            for x in range(PX):
                total = total + got[:, x * LANES : (x + 1) * LANES] * mask
        flat[:, 0:LANES] = total

    each(chunks, first_pass)
    average = jnp.sum(flat[:, 0:LANES], axis=1, keepdims=True) / points
    flat[:, 0:LANES] = jnp.zeros((CH, LANES), F32)

    def second_pass(k):
        mask = live(k)
        total = flat[:, 0:LANES]
        for b in range(KIN):
            where = slice(b * LANES, (b + 1) * LANES)
            centred = hidden[k, :, where] - average
            hidden[k, :, where] = centred
            total = total + centred * centred * mask
        flat[:, 0:LANES] = total

    each(chunks, second_pass)
    variance = jnp.sum(flat[:, 0:LANES], axis=1, keepdims=True) / points
    inverse = lax.rsqrt(variance + EPSILON)

    if chunks > 1:
        g2[...] = jnp.zeros_like(g2)
        small[...] = jnp.zeros_like(small)
    flat[:, 0 : 2 * LANES] = jnp.zeros((CH, 2 * LANES), F32)
    flat[0:8, 2 * LANES : 3 * LANES] = jnp.zeros((8, LANES), F32)

    def main_pass(k):
        mask = live(k)

        def act_first(l, x):
            normed = hidden[k, :, at(l, x)] * inverse * gain + shift
            return normed * jax.nn.sigmoid(normed)

        stack_rows(act_first, 1, s2)
        plane_products(w2f_ref, s2, 1, h2)
        for b in range(KIN):
            where = slice(b * LANES, (b + 1) * LANES)
            pre = h2[:, where]
            act2[:, where] = (pre * jax.nn.sigmoid(pre)).astype(BF16)
        for l in range(PZ):
            where = slice(l * band, (l + 1) * band)
            tap_out[:, where] = mm(w3f_ref[...], act2[:, where])
        turned = nt(eye, batch_ref[k])
        errors = []
        lost = flat[0:8, 2 * LANES : 3 * LANES]
        for l in range(PZ):
            for x in range(PX):
                sums = {}
                for t, (dz, dx, dy) in enumerate(TAPS):
                    lz, xx = l + dz, x + dx
                    if 0 <= lz < PZ and 0 <= xx < PX:
                        piece = tap_out[t * 8 : (t + 1) * 8, at(lz, xx)]
                        sums[dy] = sums[dy] + piece if dy in sums else piece
                output = sums[0] + shifted(sums[-1], -1) + shifted(sums[1], 1)
                b = l * PX + x
                error = (output - turned[b * FIELD_ROWS + 8 : b * FIELD_ROWS + 16]) * mask
                lost = lost + error * error
                errors.append(2.0 * factor * error)
        flat[0:8, 2 * LANES : 3 * LANES] = lost

        def store(where, value):
            des[:, where] = value

        stack_taps(errors, -1, store)
        add_to(small, slice(0, CH), nt(des[...], act2[...]))
        for l in range(PZ):
            got = mm(w3b_ref[...], des[:, l * band : (l + 1) * band])
            for x in range(PX):
                where = at(l, x)
                cot = got[:, x * LANES : (x + 1) * LANES].astype(BF16).astype(F32)
                pre = h2[:, where]
                sig = jax.nn.sigmoid(pre)
                h2[:, where] = cot * (sig * (1.0 + pre * (1.0 - sig)))
        stack_rows(lambda l, x: h2[:, at(l, x)], -1, s3)
        zero = jnp.zeros((CH, LANES), BF16)
        for l in range(PZ):
            for x in range(PX):
                piece = h2[:, at(l, x)].astype(BF16)
                for n in range(9):
                    goal, gx = l + n // 3 - 1, x + n % 3 - 1
                    if 0 <= goal < PZ and 0 <= gx < PX:
                        dys[n * CH : (n + 1) * CH, at(goal, gx)] = piece
                    source, sx_at = l - n // 3 + 1, x - n % 3 + 1
                    if not (0 <= source < PZ and 0 <= sx_at < PX):
                        dys[n * CH : (n + 1) * CH, at(l, x)] = zero
        plane_products(w2b_ref, s3, -1, act_cot)
        add_to(g2, slice(None), nt(dys[...], s2[...]))
        by_gain = flat[:, 0:LANES]
        by_shift = flat[:, LANES : 2 * LANES]
        for b in range(KIN):
            where = slice(b * LANES, (b + 1) * LANES)
            cot = act_cot[:, where].astype(BF16).astype(F32)
            normal = hidden[k, :, where] * inverse
            normed = normal * gain + shift
            sig = jax.nn.sigmoid(normed)
            d_normed = cot * (sig * (1.0 + normed * (1.0 - sig)))
            by_gain = by_gain + d_normed * normal
            by_shift = by_shift + d_normed
            dn[k, :, where] = d_normed
        flat[:, 0:LANES] = by_gain
        flat[:, LANES : 2 * LANES] = by_shift

    act_cot = tap_out.at[0:CH]
    each(chunks, main_pass)
    grad_gain = jnp.sum(flat[:, 0:LANES], axis=1, keepdims=True)
    grad_shift = jnp.sum(flat[:, LANES : 2 * LANES], axis=1, keepdims=True)
    loss = jnp.sum(flat[0:8, 2 * LANES : 3 * LANES]) * factor

    from_mean = -inverse * (gain * grad_shift) / points
    from_variance = -(gain * grad_gain) * inverse * inverse / points
    scale = gain * inverse

    fixed = out_ref.shape[0] - PLANE_BASE
    out_ref[PLANE_BASE:, :] = jnp.zeros((fixed, LANES), F32)
    half = MID_ROWS // 2
    out_ref[0:MID_ROWS, :] = g2[:, 0:LANES]
    out_ref[HALF_BASE : HALF_BASE + half, 0:CH] = g2[0:half, LANES:]
    out_ref[HALF_BASE : HALF_BASE + half, CH:LANES] = g2[half:, LANES:]

    def last_pass(k):
        mask = live(k)
        for b in range(KIN):
            where = slice(b * LANES, (b + 1) * LANES)
            d_hidden = dn[k, :, where] * scale + mask * (from_mean + from_variance * hidden[k, :, where])
            act2[:, where] = d_hidden.astype(BF16)
        add_to(small, slice(CH, LANES), nt(sx[k], act2[...]))

    each(chunks, last_pass)

    both = [small[pl.ds(o, 27, stride=8), :] for o in range(6)]
    planes = [pair[:, 0:CH] for pair in both] + [pair[:, CH:LANES] for pair in both[0:3]]
    for n, plane in enumerate(planes):
        base = PLANE_BASE + (n // 2) * PLANE_STEP
        side = (n % 2) * CH
        out_ref[base : base + 27, side : side + CH] = plane
    out_ref[MISC_BASE : MISC_BASE + 1, 0:CH] = line(grad_gain)
    out_ref[MISC_BASE : MISC_BASE + 1, CH:LANES] = line(grad_shift)
    out_ref[MISC_BASE + 1 : MISC_BASE + 2, :] = jnp.full((1, LANES), loss, F32)
    sources = mine_ref.shape[0]
    devices = 2 * sources
    mid, rest, _, _ = shares(devices)
    upper_band = lax.axis_index("band") == 1
    for j in range(sources):
        pair = []
        for d in (2 * j, 2 * j + 1):
            own = out_ref[PLANE_BASE + d * rest : PLANE_BASE + (d + 1) * rest, :]
            pair.append(settled(out_ref[d * mid : (d + 1) * mid, :], own, devices))
        mine_ref[j] = jnp.where(upper_band, pair[1], pair[0]).astype(BF16)
        theirs_ref[j] = jnp.where(upper_band, pair[0], pair[1]).astype(BF16)


def settled(middle, own, devices):
    mid, rest, top, rows = shares(devices)
    high, low = two_parts(own)
    both = jnp.concatenate([middle, high.astype(F32)], axis=0)
    return jnp.concatenate([fill(both, top), fill(low.astype(F32), rows - top)], axis=0)


def pair_kernel(mine_ref, theirs_ref, out_ref):
    sources = mine_ref.shape[0]
    mid, rest, top, _ = shares(2 * sources)
    for j in range(sources):
        both = mine_ref[j].astype(F32) + theirs_ref[j].astype(F32)
        own = both[mid : mid + rest] + both[top : top + rest]
        out_ref[j] = settled(both[0:mid], own, 2 * sources).astype(BF16)


def pair_sum(mine, theirs):
    return pl.pallas_call(
        pair_kernel,
        out_shape=jax.ShapeDtypeStruct(mine.shape, BF16),
        in_specs=[VMEM] * 2,
        out_specs=VMEM,
        compiler_params=small_params(4),
        name="pair_sum",
    )(mine, theirs)


def combine_kernel(parts_ref, out_ref):
    sources = parts_ref.shape[0]
    mid, rest, top, _ = shares(2 * sources)
    total = parts_ref[0].astype(F32)
    for j in range(1, sources):
        total = total + parts_ref[j].astype(F32)
    own = total[mid : mid + rest] + total[top : top + rest]
    whole = settled(total[0:mid], own, 2 * sources).astype(BF16)
    for j in range(sources):
        out_ref[j] = whole


def combine(parts):
    return pl.pallas_call(
        combine_kernel,
        out_shape=jax.ShapeDtypeStruct(parts.shape, BF16),
        in_specs=[VMEM],
        out_specs=VMEM,
        compiler_params=small_params(8),
        name="combine",
    )(parts)


def train(factor, devices, count, batch, gain, shift, weights):
    chunks = batch.shape[0]
    width = KIN * LANES
    return pl.pallas_call(
        functools.partial(train_kernel, factor),
        out_shape=(jax.ShapeDtypeStruct((devices // 2, shares(devices)[3], LANES), BF16),) * 2,
        in_specs=[SMEM] + [VMEM] * 8,
        out_specs=(VMEM,) * 2,
        scratch_shapes=[
            pltpu.VMEM((chunks, TAP_ROWS, width), BF16),
            pltpu.VMEM((chunks, CH, width), F32),
            pltpu.VMEM((3 * CH, width), BF16),
            pltpu.VMEM((3 * CH, width), BF16),
            pltpu.VMEM((CH, width), F32),
            pltpu.VMEM((CH, width), BF16),
            pltpu.VMEM((TAP_ROWS, width), F32),
            pltpu.VMEM((TAP_ROWS, width), BF16),
            pltpu.VMEM((9 * CH, width), BF16),
            pltpu.VMEM((chunks, CH, width), F32),
            pltpu.VMEM((CH, 3 * LANES), F32),
            pltpu.VMEM((9 * CH, 3 * CH), F32),
            pltpu.VMEM((TAP_ROWS, LANES), F32),
            pltpu.VMEM((padded_rows(devices)[1], LANES), F32),
        ],
        compiler_params=small_params(20 + 4 * chunks),
        name="train_step",
    )(count, batch, gain, shift, *weights)


def update_kernel(
    mine_ref, theirs_ref, wf_ref, gain_ref, shift_ref, wm_ref, wl_ref,
    nf_ref, ng_ref, ns_ref, nm_ref, nl_ref, loss_ref, grad_ref,
):
    sources = mine_ref.shape[0]
    mid, rest, top, _ = shares(2 * sources)
    upper_band = lax.axis_index("band") == 1
    for j in range(sources):
        mine, theirs = mine_ref[j].astype(F32), theirs_ref[j].astype(F32)
        pair = (jnp.where(upper_band, theirs, mine), jnp.where(upper_band, mine, theirs))
        for d, share in zip((2 * j, 2 * j + 1), pair):
            grad_ref[d * mid : (d + 1) * mid, :] = share[0:mid]
    for j in range(sources):
        mine, theirs = mine_ref[j].astype(F32), theirs_ref[j].astype(F32)
        pair = (jnp.where(upper_band, theirs, mine), jnp.where(upper_band, mine, theirs))
        for d, share in zip((2 * j, 2 * j + 1), pair):
            own = share[mid : mid + rest] + share[top : top + rest]
            grad_ref[PLANE_BASE + d * rest : PLANE_BASE + (d + 1) * rest, :] = own
    half = MID_ROWS // 2
    fold = grad_ref[HALF_BASE : HALF_BASE + half, :]
    last = jnp.concatenate([fold[:, :CH], fold[:, CH:]], axis=0)
    for zx in range(9):
        rows_at = slice(zx * CH, (zx + 1) * CH)
        block = grad_ref[rows_at, :]
        nm_ref[zx * 3] = wm_ref[zx * 3] - LEARNING * block[:, :CH]
        nm_ref[zx * 3 + 1] = wm_ref[zx * 3 + 1] - LEARNING * block[:, CH:]
        nm_ref[zx * 3 + 2] = wm_ref[zx * 3 + 2] - LEARNING * last[rows_at]
    for n in range(9):
        base = PLANE_BASE + (n // 2) * PLANE_STEP
        side = (n % 2) * CH
        plane = grad_ref[base : base + 27, side : side + CH]
        if n < 6:
            nl_ref[n] = wl_ref[n] - LEARNING * plane
        else:
            nf_ref[n - 6] = wf_ref[n - 6] - LEARNING * plane
    misc = grad_ref[MISC_BASE : MISC_BASE + 1, :]
    ng_ref[...] = gain_ref[...] - LEARNING * misc[:, :CH]
    ns_ref[...] = shift_ref[...] - LEARNING * misc[:, CH:]
    loss_ref[...] = grad_ref[MISC_BASE + 1 : MISC_BASE + 2, 0:1]


def update(mine, theirs, wf, gain, shift, wm, wl):
    shapes = [wf, gain, shift, wm, wl]
    return pl.pallas_call(
        update_kernel,
        out_shape=tuple(jax.ShapeDtypeStruct(w.shape, F32) for w in shapes) + (jax.ShapeDtypeStruct((1, 1), F32),),
        in_specs=[VMEM] * 7,
        out_specs=(VMEM,) * 6,
        scratch_shapes=[pltpu.VMEM((padded_rows(2 * mine.shape[0])[1], LANES), F32)],
        compiler_params=small_params(12),
        name="update",
    )(mine, theirs, *shapes)


def exchange(rows):
    return lax.all_to_all(rows, "sec", split_axis=0, concat_axis=0, tiled=True)


def other_band(rows):
    return lax.ppermute(rows, "band", [(0, 1), (1, 0)])


def on_device(
    velocity, crop_level, crop_x, crop_y, live_count, w_first, norm_gain, norm_shift, w_middle, w_last
):
    sources = lax.axis_size("sec")
    bands = lax.axis_size("band")
    assert bands == 2 and sources % 2 == 0
    groups = sources * bands
    wf = jnp.transpose(w_first, (2, 0, 1))
    wl = jnp.transpose(w_last, (1, 0, 2))
    weights = arrange_weights(wf, w_middle, wl)

    held, near, far, plane = edges_step(velocity)
    first = lax.ppermute(near, "sec", [(i, i ^ 1) for i in range(sources)])
    second = lax.ppermute(far, "sec", [(i, ((i + 1) ^ 1) - 1) for i in range(1, sources - 1)])
    beyond = other_band(plane)

    inner = inner_step(crop_level, crop_x, crop_y, held)
    edges = (near, far, plane, first, second, beyond)
    crops = cut_crops(inner, edges)
    velocity_next = finish_step(inner, edges)
    crops = crops.reshape(sources, PY, KIN * FIELD_ROWS)
    batch = lax.all_to_all(crops, "sec", split_axis=0, concat_axis=0, tiled=True)
    batch, velocity_next = lax.optimization_barrier((batch, velocity_next))
    batch = batch.reshape(sources // CHUNK, LANES, KIN * FIELD_ROWS)
    factor = 1.0 / (6.0 * PZ * PX * PY * (groups * sources * 5 // 8))
    gain, shift = norm_gain.reshape(1, CH), norm_shift.reshape(1, CH)
    mine, theirs = train(factor, groups, live_count, batch, gain, shift, weights)
    mine = exchange(combine(exchange(pair_sum(mine, other_band(theirs)))))
    nf, ng, ns, nm, nl, loss = update(mine, other_band(mine), wf, gain, shift, w_middle, wl)
    return (
        velocity_next,
        jnp.transpose(nf, (1, 2, 0)),
        ng.reshape(CH),
        ns.reshape(CH),
        nm,
        jnp.transpose(nl, (1, 0, 2)),
        loss.reshape(()),
    )


def solution(mesh):
    in_specs = (
        P(None, "band", "sec", None),
        P("sec", "band", None),
        P("sec", "band", None),
        P("sec", "band", None),
        P(("sec", "band")),
        P(),
        P(),
        P(),
        P(),
        P(),
    )
    out_specs = (P(None, "band", "sec", None), P(), P(), P(), P(), P(), P())
    return jax.shard_map(
        on_device, mesh=mesh, in_specs=in_specs, out_specs=out_specs, check_vma=False
    )
```

```python
import functools

import jax
import jax.numpy as jnp
from jax import lax
from jax.experimental import pallas as pl
from jax.experimental.pallas import tpu as pltpu
from jax.sharding import PartitionSpec as P

PZ = 4
PX = 4
PY = 8
CH = 64
LANES = 128
KIN = PZ * PX
CHUNK = LANES // PY
FIELD_ROWS = 16
TAP_ROWS = 27 * 8

TIME_STEP = 0.2
VISCOSITY = 0.5
LEARNING = 1.0
EPSILON = 1e-05
PAIRS = ((0, 0), (1, 1), (2, 2), (0, 1), (0, 2), (1, 2))
OFFSETS = (-1, 0, 1)
TAPS = [(dz, dx, dy) for dz in OFFSETS for dx in OFFSETS for dy in OFFSETS]

F32 = jnp.float32
BF16 = jnp.bfloat16
VMEM = pl.BlockSpec(memory_space=pltpu.VMEM)
SMEM = pl.BlockSpec(memory_space=pltpu.SMEM)
HBM = pl.BlockSpec(memory_space=pltpu.HBM)


def small_params(mib):
    return pltpu.CompilerParams(vmem_limit_bytes=min(mib, 60) * 1024 * 1024)


MID_ROWS = 9 * CH
HALF_BASE = MID_ROWS
PLANE_BASE = HALF_BASE + MID_ROWS // 2
PLANE_STEP = 32
PLANE_ROWS = 5 * PLANE_STEP
MISC_BASE = PLANE_BASE + 4 * PLANE_STEP + 27


def nt(left, right):
    return lax.dot_general(left, right, (((1,), (1,)), ((), ())), preferred_element_type=F32)


def mm(left, right):
    return lax.dot_general(left, right, (((1,), (0,)), ((), ())), preferred_element_type=F32)


def tn(left, right):
    return lax.dot_general(left, right, (((0,), (0,)), ((), ())), preferred_element_type=F32)


def shares(devices):
    mid, rest = -(-PLANE_BASE // devices), -(-PLANE_ROWS // devices)
    top = -(-(mid + rest) // 8) * 8
    return mid, rest, top, top + -(-rest // 8) * 8


def padded_rows(devices):
    mid, rest, _, _ = shares(devices)
    return devices * mid, max(PLANE_BASE + PLANE_ROWS, devices * mid, PLANE_BASE + devices * rest)


def two_parts(value):
    high = value.astype(BF16)
    return high, (value - high.astype(F32)).astype(BF16)


def fill(value, rows):
    missing = rows - value.shape[0]
    return jnp.concatenate([value, jnp.zeros((missing, LANES), F32)], axis=0) if missing else value


def each(number, body):
    if number == 1:
        body(0)
    else:
        lax.fori_loop(0, number, lambda i, c: (body(i), c)[1], 0)


def weights_kernel(wf_ref, wm_ref, wl_ref, w1_ref, w2f_ref, w2b_ref, w3f_ref, w3b_ref, goal_ref, rows):
    rows[...] = jnp.zeros_like(rows)
    for c in range(3):
        rows[pl.ds(c, 27, stride=8), :] = wf_ref[c]
    w1_ref[...] = jnp.transpose(rows[...]).astype(BF16)
    rows[...] = jnp.zeros_like(rows)
    for o in range(6):
        rows[pl.ds(o, 27, stride=8), :] = wl_ref[o]
    w3f_ref[...] = rows[...].astype(BF16)
    w3b_ref[...] = jnp.transpose(rows[...]).astype(BF16)
    for zx in range(9):
        taps = [wm_ref[zx * 3 + i] for i in range(3)]
        rows_at = slice(zx * CH, (zx + 1) * CH)
        w2f_ref[rows_at, :] = jnp.concatenate(taps, axis=1).astype(BF16)
        w2b_ref[rows_at, :] = jnp.transpose(jnp.concatenate(taps, axis=0)).astype(BF16)
    ch_rows = 9 * PZ * 8
    r = lax.broadcasted_iota(jnp.int32, (ch_rows, KIN * FIELD_ROWS), 0)
    col = lax.broadcasted_iota(jnp.int32, (ch_rows, KIN * FIELD_ROWS), 1)
    channel = r >> 5
    slot = jnp.where(channel < 3, channel, channel + 5)
    goal = ((((r >> 3) & 3) * PX + ((r & 7) >> 1)) * FIELD_ROWS) + slot
    goal_ref[...] = jnp.where((col == goal) & ((r & 1) == 0), 1.0, 0.0).astype(BF16)


def arrange_weights(wf, wm, wl):
    return pl.pallas_call(
        weights_kernel,
        out_shape=(
            jax.ShapeDtypeStruct((CH, TAP_ROWS), BF16),
            jax.ShapeDtypeStruct((9 * CH, 3 * CH), BF16),
            jax.ShapeDtypeStruct((9 * CH, 3 * CH), BF16),
            jax.ShapeDtypeStruct((TAP_ROWS, CH), BF16),
            jax.ShapeDtypeStruct((CH, TAP_ROWS), BF16),
            jax.ShapeDtypeStruct((9 * PZ * 8, KIN * FIELD_ROWS), BF16),
        ),
        in_specs=[VMEM] * 3,
        out_specs=(VMEM,) * 6,
        scratch_shapes=[pltpu.VMEM((TAP_ROWS, CH), F32)],
        compiler_params=small_params(6),
        name="arrange_weights",
    )(wf, wm, wl)


def lane_values(values_ref, which_row, base, lanes):
    which = (lanes % LANES) // PY
    out = jnp.zeros(lanes.shape, jnp.int32)
    for k in range(CHUNK):
        out = jnp.where(which == k, values_ref[which_row, 0, base + k], out)
    return out


def fold_parts(got, rows):
    return (got[0:rows] + got[rows : 2 * rows]) + got[2 * rows : 3 * rows]


def shift_down(items, offset, wanted):
    step = 1 << (len(items) - wanted).bit_length()
    while step > 1:
        step //= 2
        keep = min(len(items), wanted + step - 1)
        chosen = (offset & step) != 0
        items = [
            jnp.where(chosen, items[i + step], items[i]) if i + step < len(items) else items[i] for i in range(keep)
        ]
    return items


def x_window(cells, x_of):
    kept = cells[0 : 2 * PX]
    for o in range(1, cells.shape[0] // 2 - PX + 1):
        kept = jnp.where(x_of == o, cells[2 * o : 2 * o + 2 * PX], kept)
    return kept


def three_parts(value):
    high = value.astype(BF16)
    rest = value - high.astype(F32)
    middle = rest.astype(BF16)
    low = (rest - middle.astype(F32)).astype(BF16)
    return jnp.concatenate([high, middle, low], axis=0)


def edges_kernel(source_ref, v_ref, near_ref, far_ref, plane_ref, loads):
    odd = lax.axis_index("sec") % 2 == 1
    upper_band = lax.axis_index("band") == 1
    _, levels, nx, ny = v_ref.shape
    pieces = loads.shape[0] // 3
    span = levels // pieces
    arrivals = []
    for n in range(3 * pieces):
        where = (n // pieces, pl.ds(n % pieces * span, span))
        arrivals.append(pltpu.make_async_copy(source_ref.at[where], v_ref.at[where], loads.at[n]))
    for arrival in arrivals:
        arrival.start()
    for c in range(3):
        for arrival in arrivals[c * pieces : (c + 1) * pieces]:
            arrival.wait()
        head = v_ref[c, :, 0, :]
        tail = v_ref[c, :, nx - 1, :]
        near_ref[c] = jnp.where(odd, head, tail)
        far_ref[c] = jnp.where(odd, tail, head)
        plane_ref[c] = jnp.where(upper_band, v_ref[c, 0], v_ref[c, levels - 1])


def in_hbm(array):
    return pltpu.with_memory_space_constraint(array, pltpu.HBM)


def edges_step(velocity):
    _, levels, nx, ny = velocity.shape
    side = jax.ShapeDtypeStruct((3, levels, ny), F32)
    return pl.pallas_call(
        edges_kernel,
        out_shape=(
            jax.ShapeDtypeStruct(velocity.shape, F32), side, side, jax.ShapeDtypeStruct((3, nx, ny), F32)
        ),
        in_specs=[HBM],
        out_specs=(VMEM,) * 4,
        scratch_shapes=[pltpu.SemaphoreType.DMA((12,))],
        compiler_params=small_params(6),
        cost_estimate=cost(10**6, 3 * 10**6),
        name="edges_step",
    )(in_hbm(velocity))


def inner_kernel(
    level_ref, cx_ref, cy_ref, v_ref, vn_ref, cells_ref, picks_ref, where_ref, parts, chosen, spots, sems
):
    _, levels, nx, ny = v_ref.shape
    chunks = cells_ref.shape[0]
    arrivals = [
        pltpu.make_async_copy(ref, spots.at[n], sems.at[n]) for n, ref in enumerate((level_ref, cx_ref, cy_ref))
    ]
    for arrival in arrivals:
        arrival.start()
    row = lax.broadcasted_iota(jnp.int32, (nx, ny), 0)
    share, slope = TIME_STEP * VISCOSITY, TIME_STEP * 0.5
    for l in range(levels):
        centre = [v_ref[c, l] for c in range(3)]
        u, v, w = [slope * field for field in centre]
        to_east = jnp.where(row == nx - 1, 0.0, share - u)
        to_west = jnp.where(row == 0, 0.0, share + u)
        to_north, to_south = share - v, share + v
        to_upper, to_lower = share - w, share + w
        nxt = []
        for c in range(3):
            mid = centre[c]
            new = (1.0 - 6.0 * share) * mid
            new = new + to_east * pltpu.roll(mid, nx - 1, 0) + to_west * pltpu.roll(mid, 1, 0)
            new = new + to_north * pltpu.roll(mid, ny - 1, 1) + to_south * pltpu.roll(mid, 1, 1)
            if l + 1 < levels:
                new = new + to_upper * v_ref[c, l + 1]
            if l > 0:
                new = new + to_lower * v_ref[c, l - 1]
            vn_ref[c, l] = new
            nxt.append(new)
        parts[l * 9 * nx : (l + 1) * 9 * nx, :] = three_parts(jnp.concatenate(nxt, axis=0))

    lanes = lax.broadcasted_iota(jnp.int32, (1, 2 * LANES), 1)
    position = lax.broadcasted_iota(jnp.int32, (ny, 2 * LANES), 0)
    half = levels // 2
    span = half * 9 * nx
    for arrival in arrivals:
        arrival.wait()

    def chunk(k):
        level_of, x_of, y_of = [lane_values(spots, n, k * CHUNK, lanes) for n in range(3)]
        where_ref[k, 0:1] = level_of
        where_ref[k, 1:2] = x_of
        source = 2 * (y_of + lanes % PY) + lanes // LANES
        picks = jnp.where(position == source, 1.0, 0.0).astype(BF16)
        picks_ref[k] = picks
        for part in range(2):
            got = mm(parts[part * span : (part + 1) * span, :], picks)
            for i in range(half):
                at = i * 9 * nx
                chosen[part * half + i] = fold_parts(got[at : at + 9 * nx], 3 * nx)
        for c in range(3):
            take = slice(c * nx, (c + 1) * nx)
            kept = shift_down([chosen[l, take, :] for l in range(levels)], level_of, PZ)
            for l in range(PZ):
                cells_ref[k, l, c] = x_window(kept[l], x_of)

    each(chunks, chunk)


def beyond_terms(near_ref, far_ref, plane_ref, first_ref, second_ref, beyond_ref):
    odd = lax.axis_index("sec") % 2 == 1
    upper_band = lax.axis_index("band") == 1
    share = TIME_STEP * VISCOSITY
    slope = TIME_STEP * 0.5
    u_near, u_far, w_plane = near_ref[0], far_ref[0], plane_ref[2]
    at_west = share + slope * jnp.where(odd, u_near, u_far)
    at_east = share - slope * jnp.where(odd, u_far, u_near)
    at_plane = jnp.where(upper_band, share + slope * w_plane, share - slope * w_plane)
    west, east, plane = [], [], []
    for c in range(3):
        west.append(jnp.where(odd, first_ref[c], second_ref[c]) * at_west)
        east.append(jnp.where(odd, second_ref[c], first_ref[c]) * at_east)
        plane.append(beyond_ref[c] * at_plane)
    return upper_band, west, east, plane


def crop_kernel(
    where_ref, cells_ref, picks_ref, goal_ref, near_ref, far_ref, plane_ref, first_ref, second_ref, beyond_ref, crop_ref
):
    upper_band, west, east, plane = beyond_terms(near_ref, far_ref, plane_ref, first_ref, second_ref, beyond_ref)
    chunks = cells_ref.shape[0]
    levels, nx = west[0].shape[0], plane[0].shape[0]
    last_level, last_x = levels - PZ, nx // 2 - PX
    terms = three_parts(jnp.concatenate(west + east + plane, axis=0))
    lanes = lax.broadcasted_iota(jnp.int32, (1, 2 * LANES), 1)
    row = lax.broadcasted_iota(jnp.int32, (2 * PX, 2 * LANES), 0)

    def chunk(k):
        level_of = where_ref[k, 0:1]
        x_of = where_ref[k, 1:2]
        got = fold_parts(mm(terms, picks_ref[k]), 6 * levels + 3 * nx)
        window = [[None] * 3 for _ in range(PZ)]
        low_plane = upper_band & (level_of == 0)
        high_plane = jnp.logical_not(upper_band) & (level_of == last_level)
        for c in range(3):
            sides = []
            for side in (c, 3 + c):
                kept = got[side * levels : (side + 1) * levels]
                step = 1 << last_level.bit_length()
                while step > 1:
                    step //= 2
                    kept = jnp.where((level_of & step) != 0, pltpu.roll(kept, levels - step, 0), kept)
                sides.append(kept)
            at_west = jnp.where(x_of == 0, sides[0], 0.0)
            at_east = jnp.where(x_of == last_x, sides[1], 0.0)
            at_plane = x_window(got[6 * levels + c * nx : 6 * levels + (c + 1) * nx], x_of)
            for l in range(PZ):
                outer = jnp.where(row == 0, at_west[l : l + 1], 0.0) + jnp.where(
                    row == 2 * PX - 1, at_east[l : l + 1], 0.0
                )
                value = cells_ref[k, l, c] + outer
                if l == 0:
                    value = value + jnp.where(low_plane, at_plane, 0.0)
                if l == PZ - 1:
                    value = value + jnp.where(high_plane, at_plane, 0.0)
                window[l][c] = value

        def box(cells):
            pair = cells[:, :LANES] + cells[:, LANES:]
            return (pair + pltpu.roll(pair, 2 * PX - 1, 0)) * 0.25

        rows = [None] * (9 * PZ)
        for l in range(PZ):
            means = [box(cells) for cells in window[l]]
            for c in range(3):
                rows[c * PZ + l] = means[c]
            for n, (i, j) in enumerate(PAIRS):
                rows[(3 + n) * PZ + l] = box(window[l][i] * window[l][j]) - means[i] * means[j]
        fields = jnp.concatenate(rows, axis=0).astype(BF16)
        crop_ref[k] = tn(fields, goal_ref[...]).astype(BF16)

    each(chunks, chunk)


def finish_kernel(
    vn_ref, near_ref, far_ref, plane_ref, first_ref, second_ref, beyond_ref, out_ref, done, sems
):
    upper_band, west, east, plane = beyond_terms(near_ref, far_ref, plane_ref, first_ref, second_ref, beyond_ref)
    _, levels, nx, ny = vn_ref.shape
    row = lax.broadcasted_iota(jnp.int32, (nx, ny), 0)
    copies = []
    for l in range(levels):
        for c in range(3):
            value = vn_ref[c, l] + jnp.where(
                row == 0, west[c][l : l + 1], jnp.where(row == nx - 1, east[c][l : l + 1], 0.0)
            )
            if l == 0:
                value = value + jnp.where(upper_band, plane[c], 0.0)
            if l == levels - 1:
                value = value + jnp.where(upper_band, 0.0, plane[c])
            done[c, l] = value
        copy = pltpu.make_async_copy(done.at[:, l], out_ref.at[:, l], sems.at[l])
        copy.start()
        copies.append(copy)
    for copy in copies:
        copy.wait()


def cost(flops, moved):
    return pl.CostEstimate(flops=flops, bytes_accessed=moved, transcendentals=0)


def inner_step(level, cx, cy, velocity):
    samples = level.size
    chunks = samples // CHUNK
    _, levels, nx, ny = velocity.shape
    return pl.pallas_call(
        inner_kernel,
        out_shape=(
            jax.ShapeDtypeStruct(velocity.shape, F32),
            jax.ShapeDtypeStruct((chunks, PZ, 3, 2 * PX, 2 * LANES), F32),
            jax.ShapeDtypeStruct((chunks, ny, 2 * LANES), BF16),
            jax.ShapeDtypeStruct((chunks, 8, 2 * LANES), jnp.int32),
        ),
        in_specs=[HBM, HBM, HBM, VMEM],
        out_specs=(VMEM,) * 4,
        scratch_shapes=[
            pltpu.VMEM((levels * 9 * nx, ny), BF16),
            pltpu.VMEM((levels, 3 * nx, 2 * LANES), F32),
            pltpu.SMEM((3, 1, samples), jnp.int32),
            pltpu.SemaphoreType.DMA((3,)),
        ],
        compiler_params=small_params(14 + 2 * chunks),
        cost_estimate=cost(3 * 10**9, 8 * 10**6),
        name="inner_step",
    )(*[in_hbm(x.reshape(1, samples)) for x in (level, cx, cy)], velocity)


def cut_crops(inner, goal, edges):
    _, cells, picks, where = inner
    chunks = cells.shape[0]
    return pl.pallas_call(
        crop_kernel,
        out_shape=jax.ShapeDtypeStruct((chunks, LANES, KIN * FIELD_ROWS), BF16),
        in_specs=[VMEM] * 10,
        out_specs=VMEM,
        compiler_params=small_params(6 + 2 * chunks),
        cost_estimate=cost(10**9, 3 * 10**6),
        name="cut_crops",
    )(where, cells, picks, goal, *edges)


def finish_step(inner, edges):
    vn = inner[0]
    return pl.pallas_call(
        finish_kernel,
        out_shape=jax.ShapeDtypeStruct(vn.shape, F32),
        in_specs=[VMEM] * 7,
        out_specs=HBM,
        scratch_shapes=[pltpu.VMEM(vn.shape, F32), pltpu.SemaphoreType.DMA((vn.shape[1],))],
        compiler_params=small_params(10),
        cost_estimate=cost(2 * 10**9, 4 * 10**6),
        name="finish_step",
    )(vn, *edges)


def train_kernel(
    factor, count_ref, batch_ref, gain_ref, shift_ref, w1_ref, w2f_ref, w2b_ref, w3f_ref, w3b_ref,
    mine_ref, theirs_ref, sx, hidden, s2, s3, h2, act2, tap_out, des, dys, dn, flat, g2, small, out_ref,
):
    chunks = batch_ref.shape[0]
    width = KIN * LANES
    band = PX * LANES
    count = count_ref[0]
    points = count.astype(F32) * (KIN * PY)
    lane = lax.broadcasted_iota(jnp.int32, (1, LANES), 1)
    y = lane % PY
    inside = {-1: y > 0, 1: y < PY - 1}

    def live(k):
        return jnp.where(k * CHUNK + lane // PY < count, 1.0, 0.0)

    def shifted(block, dy):
        if dy == 0:
            return block
        return jnp.where(inside[dy], pltpu.roll(block, (-dy) % LANES, 1), 0.0)

    def at(l, x):
        return slice((l * PX + x) * LANES, (l * PX + x + 1) * LANES)

    def stack_taps(blocks, sign, store):
        moved = {dy: [shifted(block, dy) for block in blocks] for dy in OFFSETS}
        zero = jnp.zeros((8, LANES), F32)
        for l in range(PZ):
            for x in range(PX):
                column = []
                for dz, dx, dy in TAPS:
                    lz, xx = l + sign * dz, x + sign * dx
                    ok = 0 <= lz < PZ and 0 <= xx < PX
                    column.append(moved[sign * dy][lz * PX + xx] if ok else zero)
                store(at(l, x), jnp.concatenate(column, axis=0).astype(BF16))

    def stack_rows(block_of, sign, stack):
        for l in range(PZ):
            for x in range(PX):
                block = block_of(l, x)
                for i, dy in enumerate(OFFSETS):
                    stack[i * CH : (i + 1) * CH, at(l, x)] = shifted(block, sign * dy).astype(BF16)

    def plane_products(weights, stack, sign, target):
        for l in range(PZ):
            got = mm(weights[...], stack[:, l * band : (l + 1) * band])
            for i, dz in enumerate(OFFSETS):
                goal = l - sign * dz
                if not 0 <= goal < PZ:
                    continue
                for x in range(PX):
                    piece = None
                    for j, dx in enumerate(OFFSETS):
                        source = x + sign * dx
                        if 0 <= source < PX:
                            n = i * 3 + j
                            term = got[n * CH : (n + 1) * CH, source * LANES : (source + 1) * LANES]
                            piece = term if piece is None else piece + term
                    if l == max(0, goal - 1):
                        target[:, at(goal, x)] = piece
                    else:
                        target[:, at(goal, x)] += piece

    def add_to(ref, columns, value):
        if chunks > 1:
            ref[:, columns] += value
        else:
            ref[:, columns] = value

    def column(row):
        eye = lax.broadcasted_iota(jnp.int32, (CH, CH), 0) == lax.broadcasted_iota(jnp.int32, (CH, CH), 1)
        return jnp.sum(jnp.where(eye, row, 0.0), axis=1, keepdims=True)

    def line(col):
        eye = lax.broadcasted_iota(jnp.int32, (CH, CH), 0) == lax.broadcasted_iota(jnp.int32, (CH, CH), 1)
        return jnp.sum(jnp.where(eye, col, 0.0), axis=0, keepdims=True)

    gain = column(gain_ref[...])
    shift = column(shift_ref[...])
    eye_rows = KIN * FIELD_ROWS
    eye = jnp.where(
        lax.broadcasted_iota(jnp.int32, (eye_rows, eye_rows), 0)
        == lax.broadcasted_iota(jnp.int32, (eye_rows, eye_rows), 1),
        1.0,
        0.0,
    ).astype(BF16)

    flat[:, 0:LANES] = jnp.zeros((CH, LANES), F32)

    def first_pass(k):
        turned = nt(eye, batch_ref[k])
        blocks = [turned[b * FIELD_ROWS : b * FIELD_ROWS + 8] for b in range(KIN)]

        def store(where, value):
            sx[k, :, where] = value

        stack_taps(blocks, 1, store)
        mask = live(k)
        total = flat[:, 0:LANES]
        for l in range(PZ):
            got = mm(w1_ref[...], sx[k, :, l * band : (l + 1) * band])
            hidden[k, :, l * band : (l + 1) * band] = got
            for x in range(PX):
                total = total + got[:, x * LANES : (x + 1) * LANES] * mask
        flat[:, 0:LANES] = total

    each(chunks, first_pass)
    average = jnp.sum(flat[:, 0:LANES], axis=1, keepdims=True) / points
    flat[:, 0:LANES] = jnp.zeros((CH, LANES), F32)

    def second_pass(k):
        mask = live(k)
        total = flat[:, 0:LANES]
        for b in range(KIN):
            where = slice(b * LANES, (b + 1) * LANES)
            centred = hidden[k, :, where] - average
            hidden[k, :, where] = centred
            total = total + centred * centred * mask
        flat[:, 0:LANES] = total

    each(chunks, second_pass)
    variance = jnp.sum(flat[:, 0:LANES], axis=1, keepdims=True) / points
    inverse = lax.rsqrt(variance + EPSILON)

    if chunks > 1:
        g2[...] = jnp.zeros_like(g2)
        small[...] = jnp.zeros_like(small)
    flat[:, 0 : 2 * LANES] = jnp.zeros((CH, 2 * LANES), F32)
    flat[0:8, 2 * LANES : 3 * LANES] = jnp.zeros((8, LANES), F32)

    def main_pass(k):
        mask = live(k)

        def act_first(l, x):
            normed = hidden[k, :, at(l, x)] * inverse * gain + shift
            return normed * jax.nn.sigmoid(normed)

        stack_rows(act_first, 1, s2)
        plane_products(w2f_ref, s2, 1, h2)
        for b in range(KIN):
            where = slice(b * LANES, (b + 1) * LANES)
            pre = h2[:, where]
            act2[:, where] = (pre * jax.nn.sigmoid(pre)).astype(BF16)
        for l in range(PZ):
            where = slice(l * band, (l + 1) * band)
            tap_out[:, where] = mm(w3f_ref[...], act2[:, where])
        turned = nt(eye, batch_ref[k])
        errors = []
        lost = flat[0:8, 2 * LANES : 3 * LANES]
        for l in range(PZ):
            for x in range(PX):
                sums = {}
                for t, (dz, dx, dy) in enumerate(TAPS):
                    lz, xx = l + dz, x + dx
                    if 0 <= lz < PZ and 0 <= xx < PX:
                        piece = tap_out[t * 8 : (t + 1) * 8, at(lz, xx)]
                        sums[dy] = sums[dy] + piece if dy in sums else piece
                output = sums[0] + shifted(sums[-1], -1) + shifted(sums[1], 1)
                b = l * PX + x
                error = (output - turned[b * FIELD_ROWS + 8 : b * FIELD_ROWS + 16]) * mask
                lost = lost + error * error
                errors.append(2.0 * factor * error)
        flat[0:8, 2 * LANES : 3 * LANES] = lost

        def store(where, value):
            des[:, where] = value

        stack_taps(errors, -1, store)
        for l in range(PZ):
            got = mm(w3b_ref[...], des[:, l * band : (l + 1) * band])
            for x in range(PX):
                where = at(l, x)
                cot = got[:, x * LANES : (x + 1) * LANES].astype(BF16).astype(F32)
                pre = h2[:, where]
                sig = jax.nn.sigmoid(pre)
                h2[:, where] = cot * (sig * (1.0 + pre * (1.0 - sig)))
        stack_rows(lambda l, x: h2[:, at(l, x)], -1, s3)
        zero = jnp.zeros((CH, LANES), BF16)
        for l in range(PZ):
            for x in range(PX):
                piece = h2[:, at(l, x)].astype(BF16)
                for n in range(9):
                    goal, gx = l + n // 3 - 1, x + n % 3 - 1
                    if 0 <= goal < PZ and 0 <= gx < PX:
                        dys[n * CH : (n + 1) * CH, at(goal, gx)] = piece
                    source, sx_at = l - n // 3 + 1, x - n % 3 + 1
                    if not (0 <= source < PZ and 0 <= sx_at < PX):
                        dys[n * CH : (n + 1) * CH, at(l, x)] = zero
        plane_products(w2b_ref, s3, -1, act_cot)
        add_to(g2, slice(None), nt(dys[...], s2[...]))
        add_to(small, slice(0, CH), nt(des[...], act2[...]))
        by_gain = flat[:, 0:LANES]
        by_shift = flat[:, LANES : 2 * LANES]
        for b in range(KIN):
            where = slice(b * LANES, (b + 1) * LANES)
            cot = act_cot[:, where].astype(BF16).astype(F32)
            normal = hidden[k, :, where] * inverse
            normed = normal * gain + shift
            sig = jax.nn.sigmoid(normed)
            d_normed = cot * (sig * (1.0 + normed * (1.0 - sig)))
            by_gain = by_gain + d_normed * normal
            by_shift = by_shift + d_normed
            dn[k, :, where] = d_normed
        flat[:, 0:LANES] = by_gain
        flat[:, LANES : 2 * LANES] = by_shift

    act_cot = tap_out.at[0:CH]
    each(chunks, main_pass)
    grad_gain = jnp.sum(flat[:, 0:LANES], axis=1, keepdims=True)
    grad_shift = jnp.sum(flat[:, LANES : 2 * LANES], axis=1, keepdims=True)
    loss = jnp.sum(flat[0:8, 2 * LANES : 3 * LANES]) * factor

    from_mean = -inverse * (gain * grad_shift) / points
    from_variance = -(gain * grad_gain) * inverse * inverse / points
    scale = gain * inverse

    fixed = out_ref.shape[0] - PLANE_BASE
    out_ref[PLANE_BASE:, :] = jnp.zeros((fixed, LANES), F32)
    half = MID_ROWS // 2
    out_ref[0:MID_ROWS, :] = g2[:, 0:LANES]
    out_ref[HALF_BASE : HALF_BASE + half, 0:CH] = g2[0:half, LANES:]
    out_ref[HALF_BASE : HALF_BASE + half, CH:LANES] = g2[half:, LANES:]

    def last_pass(k):
        mask = live(k)
        for b in range(KIN):
            where = slice(b * LANES, (b + 1) * LANES)
            d_hidden = dn[k, :, where] * scale + mask * (from_mean + from_variance * hidden[k, :, where])
            act2[:, where] = d_hidden.astype(BF16)
        add_to(small, slice(CH, LANES), nt(sx[k], act2[...]))

    each(chunks, last_pass)

    both = [small[pl.ds(o, 27, stride=8), :] for o in range(6)]
    planes = [pair[:, 0:CH] for pair in both] + [pair[:, CH:LANES] for pair in both[0:3]]
    for n, plane in enumerate(planes):
        base = PLANE_BASE + (n // 2) * PLANE_STEP
        side = (n % 2) * CH
        out_ref[base : base + 27, side : side + CH] = plane
    out_ref[MISC_BASE : MISC_BASE + 1, 0:CH] = line(grad_gain)
    out_ref[MISC_BASE : MISC_BASE + 1, CH:LANES] = line(grad_shift)
    out_ref[MISC_BASE + 1 : MISC_BASE + 2, :] = jnp.full((1, LANES), loss, F32)
    sources = mine_ref.shape[0]
    devices = 2 * sources
    mid, rest, _, _ = shares(devices)
    upper_band = lax.axis_index("band") == 1
    for j in range(sources):
        pair = []
        for d in (2 * j, 2 * j + 1):
            own = out_ref[PLANE_BASE + d * rest : PLANE_BASE + (d + 1) * rest, :]
            pair.append(settled(out_ref[d * mid : (d + 1) * mid, :], own, devices))
        mine_ref[j] = jnp.where(upper_band, pair[1], pair[0]).astype(BF16)
        theirs_ref[j] = jnp.where(upper_band, pair[0], pair[1]).astype(BF16)


def settled(middle, own, devices):
    mid, rest, top, rows = shares(devices)
    high, low = two_parts(own)
    both = jnp.concatenate([middle, high.astype(F32)], axis=0)
    return jnp.concatenate([fill(both, top), fill(low.astype(F32), rows - top)], axis=0)


def pair_kernel(mine_ref, theirs_ref, out_ref):
    sources = mine_ref.shape[0]
    mid, rest, top, _ = shares(2 * sources)
    for j in range(sources):
        both = mine_ref[j].astype(F32) + theirs_ref[j].astype(F32)
        own = both[mid : mid + rest] + both[top : top + rest]
        out_ref[j] = settled(both[0:mid], own, 2 * sources).astype(BF16)


def pair_sum(mine, theirs):
    return pl.pallas_call(
        pair_kernel,
        out_shape=jax.ShapeDtypeStruct(mine.shape, BF16),
        in_specs=[VMEM] * 2,
        out_specs=VMEM,
        compiler_params=small_params(4),
        name="pair_sum",
    )(mine, theirs)


def combine_kernel(parts_ref, out_ref):
    sources = parts_ref.shape[0]
    mid, rest, top, _ = shares(2 * sources)
    total = parts_ref[0].astype(F32)
    for j in range(1, sources):
        total = total + parts_ref[j].astype(F32)
    own = total[mid : mid + rest] + total[top : top + rest]
    whole = settled(total[0:mid], own, 2 * sources).astype(BF16)
    for j in range(sources):
        out_ref[j] = whole


def combine(parts):
    return pl.pallas_call(
        combine_kernel,
        out_shape=jax.ShapeDtypeStruct(parts.shape, BF16),
        in_specs=[VMEM],
        out_specs=VMEM,
        compiler_params=small_params(8),
        name="combine",
    )(parts)


def train(factor, devices, count, batch, gain, shift, weights):
    chunks = batch.shape[0]
    width = KIN * LANES
    return pl.pallas_call(
        functools.partial(train_kernel, factor),
        out_shape=(jax.ShapeDtypeStruct((devices // 2, shares(devices)[3], LANES), BF16),) * 2,
        in_specs=[SMEM] + [VMEM] * 8,
        out_specs=(VMEM,) * 2,
        scratch_shapes=[
            pltpu.VMEM((chunks, TAP_ROWS, width), BF16),
            pltpu.VMEM((chunks, CH, width), F32),
            pltpu.VMEM((3 * CH, width), BF16),
            pltpu.VMEM((3 * CH, width), BF16),
            pltpu.VMEM((CH, width), F32),
            pltpu.VMEM((CH, width), BF16),
            pltpu.VMEM((TAP_ROWS, width), F32),
            pltpu.VMEM((TAP_ROWS, width), BF16),
            pltpu.VMEM((9 * CH, width), BF16),
            pltpu.VMEM((chunks, CH, width), F32),
            pltpu.VMEM((CH, 3 * LANES), F32),
            pltpu.VMEM((9 * CH, 3 * CH), F32),
            pltpu.VMEM((TAP_ROWS, LANES), F32),
            pltpu.VMEM((padded_rows(devices)[1], LANES), F32),
        ],
        compiler_params=small_params(20 + 4 * chunks),
        name="train_step",
    )(count, batch, gain, shift, *weights)


def update_kernel(
    mine_ref, theirs_ref, wf_ref, gain_ref, shift_ref, wm_ref, wl_ref,
    nf_ref, ng_ref, ns_ref, nm_ref, nl_ref, loss_ref, grad_ref,
):
    sources = mine_ref.shape[0]
    mid, rest, top, _ = shares(2 * sources)
    upper_band = lax.axis_index("band") == 1
    for j in range(sources):
        mine, theirs = mine_ref[j].astype(F32), theirs_ref[j].astype(F32)
        pair = (jnp.where(upper_band, theirs, mine), jnp.where(upper_band, mine, theirs))
        for d, share in zip((2 * j, 2 * j + 1), pair):
            grad_ref[d * mid : (d + 1) * mid, :] = share[0:mid]
    for j in range(sources):
        mine, theirs = mine_ref[j].astype(F32), theirs_ref[j].astype(F32)
        pair = (jnp.where(upper_band, theirs, mine), jnp.where(upper_band, mine, theirs))
        for d, share in zip((2 * j, 2 * j + 1), pair):
            own = share[mid : mid + rest] + share[top : top + rest]
            grad_ref[PLANE_BASE + d * rest : PLANE_BASE + (d + 1) * rest, :] = own
    half = MID_ROWS // 2
    fold = grad_ref[HALF_BASE : HALF_BASE + half, :]
    last = jnp.concatenate([fold[:, :CH], fold[:, CH:]], axis=0)
    for zx in range(9):
        rows_at = slice(zx * CH, (zx + 1) * CH)
        block = grad_ref[rows_at, :]
        nm_ref[zx * 3] = wm_ref[zx * 3] - LEARNING * block[:, :CH]
        nm_ref[zx * 3 + 1] = wm_ref[zx * 3 + 1] - LEARNING * block[:, CH:]
        nm_ref[zx * 3 + 2] = wm_ref[zx * 3 + 2] - LEARNING * last[rows_at]
    for n in range(9):
        base = PLANE_BASE + (n // 2) * PLANE_STEP
        side = (n % 2) * CH
        plane = grad_ref[base : base + 27, side : side + CH]
        if n < 6:
            nl_ref[n] = wl_ref[n] - LEARNING * plane
        else:
            nf_ref[n - 6] = wf_ref[n - 6] - LEARNING * plane
    misc = grad_ref[MISC_BASE : MISC_BASE + 1, :]
    ng_ref[...] = gain_ref[...] - LEARNING * misc[:, :CH]
    ns_ref[...] = shift_ref[...] - LEARNING * misc[:, CH:]
    loss_ref[...] = grad_ref[MISC_BASE + 1 : MISC_BASE + 2, 0:1]


def update(mine, theirs, wf, gain, shift, wm, wl):
    shapes = [wf, gain, shift, wm, wl]
    return pl.pallas_call(
        update_kernel,
        out_shape=tuple(jax.ShapeDtypeStruct(w.shape, F32) for w in shapes) + (jax.ShapeDtypeStruct((1, 1), F32),),
        in_specs=[VMEM] * 7,
        out_specs=(VMEM,) * 6,
        scratch_shapes=[pltpu.VMEM((padded_rows(2 * mine.shape[0])[1], LANES), F32)],
        compiler_params=small_params(12),
        name="update",
    )(mine, theirs, *shapes)


def exchange(rows):
    return lax.all_to_all(rows, "sec", split_axis=0, concat_axis=0, tiled=True)


def other_band(rows):
    return lax.ppermute(rows, "band", [(0, 1), (1, 0)])


def on_device(
    velocity, crop_level, crop_x, crop_y, live_count, w_first, norm_gain, norm_shift, w_middle, w_last
):
    sources = lax.axis_size("sec")
    bands = lax.axis_size("band")
    assert bands == 2 and sources % 2 == 0
    groups = sources * bands
    wf = jnp.transpose(w_first, (2, 0, 1))
    wl = jnp.transpose(w_last, (1, 0, 2))
    weights = arrange_weights(wf, w_middle, wl)

    held, near, far, plane = edges_step(velocity)
    first = lax.ppermute(near, "sec", [(i, i ^ 1) for i in range(sources)])
    second = lax.ppermute(far, "sec", [(i, ((i + 1) ^ 1) - 1) for i in range(1, sources - 1)])
    beyond = other_band(plane)

    inner = inner_step(crop_level, crop_x, crop_y, held)
    edges = (near, far, plane, first, second, beyond)
    crops = cut_crops(inner, weights[-1], edges)
    velocity_next = finish_step(inner, edges)
    crops = crops.reshape(sources, PY, KIN * FIELD_ROWS)
    batch = lax.all_to_all(crops, "sec", split_axis=0, concat_axis=0, tiled=True)
    batch, velocity_next = lax.optimization_barrier((batch, velocity_next))
    batch = batch.reshape(sources // CHUNK, LANES, KIN * FIELD_ROWS)
    factor = 1.0 / (6.0 * PZ * PX * PY * (groups * sources * 5 // 8))
    gain, shift = norm_gain.reshape(1, CH), norm_shift.reshape(1, CH)
    mine, theirs = train(factor, groups, live_count, batch, gain, shift, weights[:-1])
    mine = exchange(combine(exchange(pair_sum(mine, other_band(theirs)))))
    nf, ng, ns, nm, nl, loss = update(mine, other_band(mine), wf, gain, shift, w_middle, wl)
    return (
        velocity_next,
        jnp.transpose(nf, (1, 2, 0)),
        ng.reshape(CH),
        ns.reshape(CH),
        nm,
        jnp.transpose(nl, (1, 0, 2)),
        loss.reshape(()),
    )


def solution(mesh):
    in_specs = (
        P(None, "band", "sec", None),
        P("sec", "band", None),
        P("sec", "band", None),
        P("sec", "band", None),
        P(("sec", "band")),
        P(),
        P(),
        P(),
        P(),
        P(),
    )
    out_specs = (P(None, "band", "sec", None), P(), P(), P(), P(), P(), P())
    return jax.shard_map(
        on_device, mesh=mesh, in_specs=in_specs, out_specs=out_specs, check_vma=False
    )
```
